512 devices in a mesh: round: 8 (over z_hi, x), tile: 64 (over z_lo, y, core).
Axes of the slice: x: 4, y: 8, z: 8 (z_hi: 2, z_lo: 4; z = z_hi * 4 + z_lo), core: 2. Of those that a mesh axis runs over, the one named last changes fastest.
Arguments:
- raw_tiles: bfloat16 [8, 4, 8, 256, 512], P('round', None, None, 'tile'), may hold values from -6 to 6
- ref_bands: bfloat16 [8, 256, 512], P('round', 'tile'), may hold values from -6 to 6
- shifts: int32 [8, 64], P('round', 'tile'), may hold values from 0 to 511
- matrix_ids: int32 [8, 4], P('round'), may hold values from 0 to 3
- resample: bfloat16 [4, 512, 512], replicated, may hold values from -0.25 to 0.25
- unmix: bfloat16 [32, 32], replicated, may hold values from -1 to 1
- conv_weight: bfloat16 [27, 64, 32], replicated, may hold values from -0.21875 to 0.21875
- conv_bias: float32 [64], replicated, may hold values from -3 to 3
- out_weight: bfloat16 [32, 64], replicated, may hold values from -0.75 to 0.75
Outputs:
- correlation: float32 [8, 4, 8, 256, 512], P('round', None, None, 'tile')
- features: bfloat16 [32, 8, 512, 256], P(None, 'round', 'tile')
The draws below stay inside these ranges and needn't reach their ends.
All inputs are finite; a program needn't handle non-finite values.
Results may differ from the reference program's by a relative error of at most 0.0059.
Values may be sent and summed in bfloat16 or wider, within the bound.
No kernel may reach another device: no remote copies, remote signals or barrier semaphores. Data moves between devices by JAX's collectives and lax.ppermute only.
A program may use at most 64 MiB of HBM per device.

```python
import math
import jax
import jax.numpy as jnp
from jax import lax

CHANNELS = 4
TABLE_SIZE = 4
HIDDEN_CH = 64
ROWS_TILE = 4
ROUNDS = 8
TILES = 64
DEPTH = 8
HEIGHT = 256
WIDTH = 512
MIXED = 32


def set_ends(drawn, rng, least, high):
    longest = drawn.shape.index(max(drawn.shape))
    spots = []
    for shift in (0, 1):
        where = [jax.random.randint(jax.random.fold_in(rng, axis), (), 0, length) for axis, length in enumerate(drawn.shape)]
        where[longest] = (where[longest] + shift) % drawn.shape[longest]
        spots.append(tuple(where))
    return drawn.at[spots[0]].set(least).at[spots[1]].set(high)


def shard_levels(rng, dims, cuts, smallest, largest):
    loudness, own = 1.0, jax.random.fold_in(rng, 6)
    for axis_at, blocks in cuts:
        draws = jnp.exp(jax.random.uniform(jax.random.fold_in(own, axis_at), (blocks,), jnp.float32, smallest / len(cuts), largest / len(cuts)))
        loudness = loudness * jnp.repeat(draws, dims[axis_at] // blocks).reshape([-1 if axis == axis_at else 1 for axis in range(len(dims))])
    return loudness


def centred(rng, dims, scale, reach, shards=(), held_as=jnp.bfloat16):
    result = jax.random.normal(rng, dims, jnp.float32) * scale
    if len(shards) > 0:
        result = shard_levels(rng, dims, shards, -0.22, 0.18) * result
    return jnp.clip(result, min=-reach, max=reach).astype(held_as)


def setup_inputs(seed: int = 0) -> dict:
    key_of = jax.random.split(jax.random.key(seed), 10)
    return {
        "raw_tiles": centred(key_of[0], (ROUNDS, CHANNELS, DEPTH, HEIGHT, WIDTH), 1.0, 6.0, ((0, 8), (3, 64))),
        "ref_bands": centred(key_of[1], (DEPTH, HEIGHT, WIDTH), 1.0, 6.0, ((0, 8), (1, 64))),
        "shifts": set_ends(jax.random.randint(key_of[2], (ROUNDS, TILES), 0, WIDTH), jax.random.fold_in(key_of[2], 1), 0, WIDTH - 1).astype(jnp.int32),
        "matrix_ids": set_ends(jax.random.randint(key_of[3], (ROUNDS, CHANNELS), 0, TABLE_SIZE), jax.random.fold_in(key_of[3], 1), 0, TABLE_SIZE - 1).astype(jnp.int32),
        "resample": centred(key_of[4], (TABLE_SIZE, WIDTH, WIDTH), WIDTH ** -0.5, 0.25),
        "unmix": centred(key_of[5], (MIXED, MIXED), MIXED ** -0.5, 1.0),
        "conv_weight": centred(key_of[6], (27, HIDDEN_CH, MIXED), (27 * MIXED) ** -0.5, 0.21875),
        "conv_bias": centred(key_of[7], (HIDDEN_CH,), 0.5, 3.0, (), jnp.float32),
        "out_weight": centred(key_of[8], (MIXED, HIDDEN_CH), HIDDEN_CH ** -0.5, 0.75),
    }


def reference(raw_tiles, ref_bands, shifts, matrix_ids, resample, unmix, conv_weight, conv_bias, out_weight):
    columns = jnp.arange(WIDTH, dtype=jnp.int32)
    band_spectra = jnp.fft.rfft(ref_bands.astype(jnp.float32), axis=-1)

    def one_round(operands):
        raw_round, shift_row, id_row = operands
        sources = (columns[None, :] - shift_row[:, None]) % WIDTH
        sources = jnp.broadcast_to(sources[None, None, :, None, :], (CHANNELS, DEPTH, TILES, ROWS_TILE, WIDTH)).astype(jnp.int32)
        tiled = raw_round.reshape(CHANNELS, DEPTH, TILES, ROWS_TILE, WIDTH)
        shifted = jnp.take_along_axis(tiled, sources, axis=4).reshape(CHANNELS, DEPTH, HEIGHT, WIDTH)
        matrices = resample[id_row].astype(jnp.float32)
        warped = jnp.einsum('czyx,cxw->czyw', shifted.astype(jnp.float32), matrices).astype(jnp.bfloat16)
        spectra = jnp.fft.rfft(warped.astype(jnp.float32), axis=-1)
        product = spectra * jnp.conj(band_spectra)[None]
        correlation = jnp.fft.irfft(product, n=WIDTH, axis=-1) / math.sqrt(WIDTH)
        return (warped, correlation.astype(jnp.float32))
    warped, correlation = lax.map(one_round, (raw_tiles, shifts, matrix_ids))
    bricks = jnp.transpose(warped.reshape(MIXED, DEPTH, HEIGHT, WIDTH), (0, 1, 3, 2))
    unmixed = jnp.einsum('ji,izxy->jzxy', unmix.astype(jnp.float32), bricks.astype(jnp.float32)).astype(jnp.bfloat16)
    padded = jnp.pad(unmixed, ((0, 0), (1, 1), (1, 1), (1, 1)))
    weights = conv_weight.astype(jnp.float32)
    out_matrix = out_weight.astype(jnp.float32)
    biases = conv_bias.astype(jnp.float32)

    def one_plane(plane):
        window = lax.dynamic_slice_in_dim(padded, plane, 3, axis=1).astype(jnp.float32)
        total = jnp.zeros((HIDDEN_CH, WIDTH, HEIGHT), jnp.float32)
        for offset in range(27):
            step_z = offset // 9
            step_x = offset // 3 % 3
            step_y = offset % 3
            total = total + jnp.einsum('hc,cxy->hxy', weights[offset], window[:, step_z, step_x:step_x + WIDTH, step_y:step_y + HEIGHT])
        hidden = jax.nn.gelu(total + biases[:, None, None]).astype(jnp.bfloat16)
        return jnp.einsum('ch,hxy->cxy', out_matrix, hidden.astype(jnp.float32))
    mixed_back = lax.map(one_plane, jnp.arange(DEPTH, dtype=jnp.int32))
    features = (unmixed.astype(jnp.float32) + jnp.transpose(mixed_back, (1, 0, 2, 3))).astype(jnp.bfloat16)
    return (correlation, features)
```

```python
import functools
import math

import jax
import jax.numpy as jnp
import numpy as np
from jax import lax
from jax.experimental import pallas as pl
from jax.experimental.pallas import tpu as pltpu
from jax.sharding import PartitionSpec as P

BF = jnp.bfloat16
F32 = jnp.float32
ROUNDS, TILES = 8, 64
CH, DEPTH, ROWS, WIDTH = 4, 8, 4, 512
MIXED, HIDDEN = 32, 64
PLANE = CH * ROWS
CHUNK = 3 * PLANE + 2 * ROWS
BRICK = WIDTH // TILES


def iota(shape, dim):
    return lax.broadcasted_iota(jnp.int32, shape, dim)


def dot(a, b, dims):
    return lax.dot_general(a, b, (dims, ((), ())), preferred_element_type=F32)


def warp_kernel(shift, ids, raw, band, table, out, mats, sems):
    copies = [
        pltpu.make_async_copy(table.at[ids[0, c]], mats.at[c], sems.at[c]) for c in range(CH)
    ]
    for copy in copies:
        copy.start()
    by = shift[0, 0]
    warped = []
    for c in range(CH):
        rows = jnp.concatenate([raw[c, z].astype(F32) for z in range(DEPTH)], axis=0)
        rows = pltpu.roll(rows, by, 1).astype(BF)
        copies[c].wait()
        result = dot(rows, mats[c], ((1,), (0,)))
        warped.append(result.reshape(DEPTH // 2, 2 * ROWS, WIDTH))
    low = iota((DEPTH // 2, 2 * ROWS, WIDTH), 1) < ROWS
    even, odd = [], []
    for c in range(0, CH, 2):
        a, b = warped[c], warped[c + 1]
        even.append(jnp.where(low, a, pltpu.roll(b, ROWS, 1)))
        odd.append(jnp.where(low, pltpu.roll(a, ROWS, 1), b))
    for z in range(DEPTH):
        parts = odd if z % 2 else even
        plane = jnp.concatenate([p[z // 2] for p in parts], axis=0).astype(BF)
        for side in range(3):
            peer = z + 1 - side
            if 0 <= peer < DEPTH:
                out[peer, side * PLANE : (side + 1) * PLANE, :] = plane
    nothing = jnp.zeros((PLANE, WIDTH), BF)
    out[0, :PLANE, :] = nothing
    out[DEPTH - 1, 2 * PLANE : 3 * PLANE, :] = nothing
    own = band[...].astype(F32)
    own = jnp.concatenate([own, own], axis=0).astype(BF)
    for peer in range(DEPTH):
        out[peer, 3 * PLANE :, :] = own


def warp(shift, ids, raw, band, table, interpret=False):
    return pl.pallas_call(
        warp_kernel,
        out_shape=jax.ShapeDtypeStruct((ROUNDS, CHUNK, WIDTH), BF),
        in_specs=[
            pl.BlockSpec(memory_space=pltpu.SMEM),
            pl.BlockSpec(memory_space=pltpu.SMEM),
            pl.BlockSpec(memory_space=pltpu.VMEM),
            pl.BlockSpec(memory_space=pltpu.VMEM),
            pl.BlockSpec(memory_space=pl.ANY),
        ],
        out_specs=pl.BlockSpec(memory_space=pltpu.VMEM),
        scratch_shapes=[pltpu.VMEM((CH, WIDTH, WIDTH), BF), pltpu.SemaphoreType.DMA((CH,))],
        name="warp",
        interpret=interpret,
    )(shift, ids, raw, band, table)


def prepare_kernel(unmix, conv, bias, project, spread, banded, biases, projected):
    n = MIXED * ROWS
    pick_in = (iota((n, MIXED), 0) // ROWS == iota((n, MIXED), 1)).astype(BF)
    pick_out = (iota((MIXED, n), 1) % MIXED == iota((MIXED, n), 0)).astype(BF)
    tall = dot(pick_in, unmix[...], ((1,), (1,))).astype(BF)
    wide = dot(tall, pick_out, ((1,), (0,)))
    own = iota((n, n), 0) % ROWS == iota((n, n), 1) // MIXED
    spread[...] = jnp.where(own, wide, 0.0).astype(BF)
    gap = jnp.zeros((HIDDEN, MIXED), BF)
    for ab in range(9):
        d = [conv[3 * ab + i] for i in range(3)]
        rows = [
            [d[1], d[2], gap, gap, gap, gap, gap, d[0]],
            [d[0], d[1], d[2], gap, gap, gap, gap, gap],
            [gap, d[0], d[1], d[2], gap, gap, gap, gap],
            [gap, gap, d[0], d[1], d[2], gap, gap, gap],
        ]
        for y in range(ROWS):
            banded[y * HIDDEN : (y + 1) * HIDDEN, ab * 256 : (ab + 1) * 256] = jnp.concatenate(
                rows[y], axis=1
            )
    biases[...] = jnp.concatenate([bias[...]] * ROWS, axis=1)
    hole = jnp.zeros((MIXED, HIDDEN), BF)
    for y in range(ROWS):
        row = [project[...] if i == y else hole for i in range(ROWS)]
        projected[y * MIXED : (y + 1) * MIXED, :] = jnp.concatenate(row, axis=1)


def prepare(unmix, conv, bias, project, interpret=False):
    return pl.pallas_call(
        prepare_kernel,
        out_shape=(
            jax.ShapeDtypeStruct((MIXED * ROWS, MIXED * ROWS), BF),
            jax.ShapeDtypeStruct((HIDDEN * ROWS, 9 * 256), BF),
            jax.ShapeDtypeStruct((1, HIDDEN * ROWS), F32),
            jax.ShapeDtypeStruct((MIXED * ROWS, HIDDEN * ROWS), BF),
        ),
        name="prepare",
        interpret=interpret,
    )(unmix, conv, bias, project)


def unmix_kernel(got, spread, out):
    shape = (TILES, BRICK, MIXED * ROWS)
    row = iota(shape, 1)
    edge = jnp.zeros((1,) + shape[1:], F32)
    planes = []
    rims = jnp.zeros(shape, F32)
    for side in range(3):
        mixed = got[:, side * PLANE : (side + 1) * PLANE, :].reshape(ROUNDS * PLANE, WIDTH)
        plane = dot(mixed, spread[...], ((0,), (0,))).reshape(shape)
        planes.append(plane)
        before = jnp.concatenate([edge, plane[:-1]], axis=0)
        after = jnp.concatenate([plane[1:], edge], axis=0)
        rims = jnp.where(row == side, pltpu.roll(before, (side + 1) % BRICK, 1), rims)
        rims = jnp.where(row == 3 + side, pltpu.roll(after, 3 + side, 1), rims)
    out[...] = jnp.concatenate(planes + [rims], axis=1).astype(BF)


def unmixed_chunks(got, spread, interpret=False):
    return pl.pallas_call(
        unmix_kernel,
        out_shape=jax.ShapeDtypeStruct((TILES, 4 * BRICK, MIXED * ROWS), BF),
        name="unmix",
        interpret=interpret,
    )(got, spread)


def tables():
    x = np.arange(WIDTH, dtype=np.int64)
    half = WIDTH // 2
    frequency = np.where(x < half, x, np.where(x == half, half, x - half))
    angles = (x[:, None] * frequency[None, :] % WIDTH) * (2.0 * math.pi / WIDTH)
    table = np.where((x <= half)[None, :], np.cos(angles), np.sin(angles)).astype(np.float32)
    high = table.astype(jnp.bfloat16)
    low = (table - high.astype(np.float32)).astype(jnp.bfloat16)
    return high, low


def correlate_kernel(sent, got, high, low, out):
    half = WIDTH // 2
    own = sent[:, PLANE : 2 * PLANE, :].reshape(DEPTH * PLANE, WIDTH)
    band = got[:, 3 * PLANE :, :].astype(F32).reshape(DEPTH * 2 * ROWS, WIDTH).astype(BF)
    rows = jnp.concatenate([own, band], axis=0)
    along = ((1,), (0,))
    spectra = dot(rows, high[...], along) + dot(rows, low[...], along)
    count = DEPTH * PLANE
    own_cos = spectra[:count, :half].reshape(DEPTH, 2, 2 * ROWS, half)
    own_sin = spectra[:count, half:].reshape(DEPTH, 2, 2 * ROWS, half)
    band_cos = spectra[count:, :half].reshape(DEPTH, 1, 2 * ROWS, half)
    band_sin = spectra[count:, half:].reshape(DEPTH, 1, 2 * ROWS, half)
    first = iota(own_cos.shape, 3) == 0
    sines = own_sin * band_sin
    cosines = own_cos * band_cos
    real = jnp.where(first, cosines, 2.0 * (cosines + sines))
    imag = jnp.where(first, sines, 2.0 * (own_sin * band_cos - own_cos * band_sin))
    joined = jnp.concatenate([real.reshape(count, half), imag.reshape(count, half)], axis=1)
    upper = joined.astype(BF)
    lower = (joined - upper.astype(F32)).astype(BF)
    across = ((1,), (1,))
    both = dot(jnp.concatenate([upper, lower], axis=0), high[...], across)
    inverse = both[:count] + both[count:] + dot(upper, low[...], across)
    inverse = inverse * (1.0 / (WIDTH * math.sqrt(WIDTH)))
    for z in range(DEPTH):
        for c in range(CH):
            start = z * PLANE + c * ROWS
            out[c, z] = inverse[start : start + ROWS]


def correlate(sent, got, high, low, interpret=False):
    return pl.pallas_call(
        correlate_kernel,
        out_shape=jax.ShapeDtypeStruct((CH, DEPTH, ROWS, WIDTH), F32),
        name="correlate",
        interpret=interpret,
    )(sent, got, high, low)


def layer_kernel(got, banded, biases, projected, out, wide, done, first, second):
    shape = (TILES, BRICK, MIXED * ROWS)
    flat = (TILES * BRICK, MIXED * ROWS)
    row = iota(shape, 1)
    right = iota(shape, 2) >= 64
    edge = jnp.zeros((1,) + shape[1:], F32)
    whole = got[...].astype(F32)
    rims = whole[:, 3 * BRICK :, :]
    centre = None
    for a in range(3):
        plane = whole[:, a * BRICK : (a + 1) * BRICK, :]
        if a == 1:
            centre = plane.reshape(flat)
        before = pltpu.roll(rims, (BRICK - a) % BRICK, 1) if a else rims
        after = pltpu.roll(rims, 4 - a, 1)
        views = (
            jnp.where(row == 0, before, pltpu.roll(plane, 1, 1)),
            plane,
            jnp.where(row == BRICK - 1, after, pltpu.roll(plane, BRICK - 1, 1)),
        )
        for b, view in enumerate(views):
            at = (3 * a + b) * 256
            upper = jnp.concatenate([edge, view[:-1]], axis=0)
            lower = jnp.concatenate([view[1:], edge], axis=0)
            wide[:, at : at + 128] = view.reshape(flat).astype(BF)
            wide[:, at + 128 : at + 256] = jnp.where(right, upper, lower).reshape(flat).astype(BF)
    total = dot(wide[...], banded[...], ((1,), (1,))) + biases[...]
    hidden = jax.nn.gelu(total).astype(BF)
    mixed = dot(hidden, projected[...], ((1,), (1,)))
    done[...] = centre + mixed
    left = iota((MIXED, 128), 1) < 64
    order = iota((256, 256), 1) == 4 * (iota((256, 256), 0) % 64) + iota((256, 256), 0) // 64
    order = order.astype(BF)
    lines = []
    for x in range(0, BRICK, 2):
        pair = jnp.concatenate(
            [done[pl.ds(x, TILES, stride=BRICK), :], done[pl.ds(x + 1, TILES, stride=BRICK), :]],
            axis=0,
        ).T
        y = [pair[i * MIXED : (i + 1) * MIXED, :] for i in range(ROWS)]
        lines.append(
            jnp.concatenate(
                [
                    jnp.where(left, y[0], pltpu.roll(y[1], 64, 1)),
                    jnp.where(left, y[2], pltpu.roll(y[3], 64, 1)),
                ],
                axis=1,
            )
        )
        lines.append(
            jnp.concatenate(
                [
                    jnp.where(left, pltpu.roll(y[0], 64, 1), y[1]),
                    jnp.where(left, pltpu.roll(y[2], 64, 1), y[3]),
                ],
                axis=1,
            )
        )
    ordered = dot(jnp.concatenate(lines, axis=0).astype(BF), order, ((1,), (0,)))
    for x in range(BRICK):
        rows = ordered[x * MIXED : (x + 1) * MIXED]
        first[pl.ds(x, MIXED, stride=BRICK), :] = rows[:, :128]
        second[pl.ds(x, MIXED, stride=BRICK), :] = rows[:, 128:]
    out[:, :, :128] = first[...].reshape(MIXED, BRICK, 128).astype(BF)
    out[:, :, 128:] = second[...].reshape(MIXED, BRICK, 128).astype(BF)


def layer(got, banded, biases, projected, interpret=False):
    return pl.pallas_call(
        layer_kernel,
        out_shape=jax.ShapeDtypeStruct((MIXED, BRICK, TILES * ROWS), BF),
        scratch_shapes=[
            pltpu.VMEM((TILES * BRICK, 9 * 256), BF),
            pltpu.VMEM((TILES * BRICK, MIXED * ROWS), F32),
            pltpu.VMEM((MIXED * BRICK, 128), F32),
            pltpu.VMEM((MIXED * BRICK, 128), F32),
        ],
        name="layer",
        interpret=interpret,
    )(got, banded, biases, projected)


def body(
    raw_tiles, ref_bands, shifts, matrix_ids, resample, unmix, conv_weight, conv_bias, out_weight
):
    high, low = tables()
    swap = functools.partial(lax.all_to_all, split_axis=0, concat_axis=0, tiled=True)
    spread, banded, biases, projected = prepare(
        unmix, conv_weight, conv_bias.reshape(1, -1), out_weight
    )
    sent = warp(shifts, matrix_ids, raw_tiles[0], ref_bands[0], resample)
    got = swap(sent, "round")
    chunks = swap(unmixed_chunks(got, spread), "tile")
    correlation = correlate(sent, got, jnp.asarray(high), jnp.asarray(low))
    features = layer(chunks, banded, biases, projected)
    return (correlation[None], features[:, None])


def solution(mesh):
    placed = (
        P("round", None, None, "tile", None),
        P("round", "tile", None),
        P("round", "tile"),
        P("round", None),
        P(),
        P(),
        P(),
        P(),
        P(),
    )
    return jax.shard_map(
        body,
        mesh=mesh,
        in_specs=placed,
        out_specs=(P("round", None, None, "tile", None), P(None, "round", "tile", None)),
        check_vma=False,
    )
```

```python
import functools
import math

import jax
import jax.numpy as jnp
import numpy as np
from jax import lax
from jax.experimental import pallas as pl
from jax.experimental.pallas import tpu as pltpu
from jax.sharding import PartitionSpec as P

BF = jnp.bfloat16
F32 = jnp.float32
ROUNDS, TILES = 8, 64
CH, DEPTH, ROWS, WIDTH = 4, 8, 4, 512
MIXED, HIDDEN = 32, 64
PLANE = CH * ROWS
CHUNK = 3 * PLANE + 2 * ROWS
BRICK = WIDTH // TILES
SPAN = BRICK + 2


def iota(shape, dim):
    return lax.broadcasted_iota(jnp.int32, shape, dim)


def dot(a, b, dims):
    return lax.dot_general(a, b, (dims, ((), ())), preferred_element_type=F32)


def warp_kernel(shift, ids, raw, table, out, own, mats, sems):
    copies = [
        pltpu.make_async_copy(table.at[ids[0, c]], mats.at[c], sems.at[c]) for c in range(CH)
    ]
    for copy in copies:
        copy.start()
    by = shift[0, 0]
    warped = []
    for c in range(CH):
        rows = jnp.concatenate([raw[c, z].astype(F32) for z in range(DEPTH)], axis=0)
        rows = pltpu.roll(rows, by, 1).astype(BF)
        copies[c].wait()
        result = dot(rows, mats[c], ((1,), (0,)))
        own[c] = result.astype(BF)
        warped.append(result.reshape(DEPTH // 2, 2 * ROWS, WIDTH))
    low = iota((DEPTH // 2, 2 * ROWS, WIDTH), 1) < ROWS
    even, odd = [], []
    for c in range(0, CH, 2):
        a, b = warped[c], warped[c + 1]
        even.append(jnp.where(low, a, pltpu.roll(b, ROWS, 1)))
        odd.append(jnp.where(low, pltpu.roll(a, ROWS, 1), b))
    planes = []
    for z in range(DEPTH):
        planes += [p[z // 2] for p in (odd if z % 2 else even)]
    upright = jnp.concatenate(planes, axis=0).T.reshape(TILES, BRICK, DEPTH * PLANE)
    edge = jnp.zeros((1, BRICK, DEPTH * PLANE), F32)
    before = jnp.concatenate([edge, upright[:-1]], axis=0)
    after = jnp.concatenate([upright[1:], edge], axis=0)
    row = iota(upright.shape, 1)
    rims = jnp.where(row == 0, pltpu.roll(before, 1, 1), pltpu.roll(after, 1, 1))
    out[...] = jnp.concatenate([upright, rims], axis=1).astype(BF)


def warp(shift, ids, raw, table, interpret=False):
    return pl.pallas_call(
        warp_kernel,
        out_shape=(
            jax.ShapeDtypeStruct((TILES, 2 * BRICK, DEPTH * PLANE), BF),
            jax.ShapeDtypeStruct((CH, DEPTH * ROWS, WIDTH), BF),
        ),
        in_specs=[
            pl.BlockSpec(memory_space=pltpu.SMEM),
            pl.BlockSpec(memory_space=pltpu.SMEM),
            pl.BlockSpec(memory_space=pltpu.VMEM),
            pl.BlockSpec(memory_space=pl.ANY),
        ],
        scratch_shapes=[pltpu.VMEM((CH, WIDTH, WIDTH), BF), pltpu.SemaphoreType.DMA((CH,))],
        name="warp",
        interpret=interpret,
    )(shift, ids, raw, table)


def prepare_kernel(unmix, conv, bias, project, spread, banded, biases, projected):
    n = MIXED * ROWS
    pick_in = (iota((n, MIXED), 0) // ROWS == iota((n, MIXED), 1)).astype(BF)
    pick_out = (iota((MIXED, n), 1) % MIXED == iota((MIXED, n), 0)).astype(BF)
    tall = dot(pick_in, unmix[...], ((1,), (1,))).astype(BF)
    wide = dot(tall, pick_out, ((1,), (0,)))
    own = iota((n, n), 0) % ROWS == iota((n, n), 1) // MIXED
    spread[...] = jnp.where(own, wide, 0.0).astype(BF)
    gap = jnp.zeros((HIDDEN, MIXED), BF)
    for ab in range(9):
        at = (ab % 3 * 3 + ab // 3) * 256
        d = [conv[3 * ab + i] for i in range(3)]
        rows = [
            [d[1], d[2], gap, gap, gap, gap, gap, d[0]],
            [d[0], d[1], d[2], gap, gap, gap, gap, gap],
            [gap, d[0], d[1], d[2], gap, gap, gap, gap],
            [gap, gap, d[0], d[1], d[2], gap, gap, gap],
        ]
        for y in range(ROWS):
            banded[y * HIDDEN : (y + 1) * HIDDEN, at : at + 256] = jnp.concatenate(
                rows[y], axis=1
            )
    biases[...] = jnp.concatenate([bias[...]] * ROWS, axis=1)
    hole = jnp.zeros((MIXED, HIDDEN), BF)
    for y in range(ROWS):
        row = [project[...] if i == y else hole for i in range(ROWS)]
        projected[y * MIXED : (y + 1) * MIXED, :] = jnp.concatenate(row, axis=1)


def prepare(unmix, conv, bias, project, interpret=False):
    return pl.pallas_call(
        prepare_kernel,
        out_shape=(
            jax.ShapeDtypeStruct((MIXED * ROWS, MIXED * ROWS), BF),
            jax.ShapeDtypeStruct((HIDDEN * ROWS, 9 * 256), BF),
            jax.ShapeDtypeStruct((1, HIDDEN * ROWS), F32),
            jax.ShapeDtypeStruct((MIXED * ROWS, HIDDEN * ROWS), BF),
        ),
        name="prepare",
        interpret=interpret,
    )(unmix, conv, bias, project)


def regroup_kernel(got, band, out, tall):
    mine = band[...].astype(F32)
    mine = jnp.concatenate([mine, mine], axis=0).astype(BF)
    for peer in range(ROUNDS):
        out[peer, 3 * PLANE :, :WIDTH] = mine
        out[peer, 3 * PLANE :, WIDTH:] = jnp.zeros((2 * ROWS, SPAN * TILES - WIDTH), BF)
    tall[...] = got[...].astype(F32).reshape(TILES * 2 * BRICK, DEPTH * PLANE)
    columns = [BRICK] + list(range(BRICK)) + [BRICK + 1]
    for pair in range(SPAN // 2):
        upright = [
            tall[pl.ds(x, TILES, stride=2 * BRICK), :] for x in columns[2 * pair : 2 * pair + 2]
        ]
        flat = jnp.concatenate(upright, axis=0).T.astype(BF)
        for z in range(DEPTH):
            for side in range(3):
                peer = z + 1 - side
                if 0 <= peer < DEPTH:
                    out[
                        peer, side * PLANE : (side + 1) * PLANE, pair * 128 : (pair + 1) * 128
                    ] = flat[z * PLANE : (z + 1) * PLANE]
    nothing = jnp.zeros((PLANE, SPAN * TILES), BF)
    out[0, :PLANE, :] = nothing
    out[DEPTH - 1, 2 * PLANE : 3 * PLANE, :] = nothing


def regroup(got, band, interpret=False):
    return pl.pallas_call(
        regroup_kernel,
        out_shape=jax.ShapeDtypeStruct((ROUNDS, CHUNK, SPAN * TILES), BF),
        scratch_shapes=[pltpu.VMEM((TILES * 2 * BRICK, DEPTH * PLANE), F32)],
        name="regroup",
        interpret=interpret,
    )(got, band)


def tables():
    x = np.arange(WIDTH, dtype=np.int64)
    half = WIDTH // 2
    frequency = np.where(x < half, x, np.where(x == half, half, x - half))
    angles = (x[:, None] * frequency[None, :] % WIDTH) * (2.0 * math.pi / WIDTH)
    table = np.where((x <= half)[None, :], np.cos(angles), np.sin(angles)).astype(np.float32)
    high = table.astype(jnp.bfloat16)
    low = (table - high.astype(np.float32)).astype(jnp.bfloat16)
    return high, low


def spectra_kernel(own, high, low, out):
    rows = own[...].reshape(CH * DEPTH * ROWS, WIDTH)
    out[...] = dot(rows, high[...], ((1,), (0,))) + dot(rows, low[...], ((1,), (0,)))


def own_spectra(own, high, low, interpret=False):
    return pl.pallas_call(
        spectra_kernel,
        out_shape=jax.ShapeDtypeStruct((CH * DEPTH * ROWS, WIDTH), F32),
        name="spectra",
        interpret=interpret,
    )(own, high, low)


def correlate_kernel(own, got, high, low, out):
    half = WIDTH // 2
    count = CH * DEPTH * ROWS
    band = jnp.concatenate(
        [got[z, 3 * PLANE :, :WIDTH].astype(F32)[:ROWS] for z in range(DEPTH)], axis=0
    ).astype(BF)
    along = ((1,), (0,))
    band = dot(band, high[...], along) + dot(band, low[...], along)
    own_cos = own[:, :half].reshape(CH, DEPTH * ROWS, half)
    own_sin = own[:, half:].reshape(CH, DEPTH * ROWS, half)
    band_cos = band[:, :half]
    band_sin = band[:, half:]
    first = iota(own_cos.shape, 2) == 0
    sines = own_sin * band_sin
    cosines = own_cos * band_cos
    real = jnp.where(first, cosines, 2.0 * (cosines + sines))
    imag = jnp.where(first, sines, 2.0 * (own_sin * band_cos - own_cos * band_sin))
    joined = jnp.concatenate([real.reshape(count, half), imag.reshape(count, half)], axis=1)
    upper = joined.astype(BF)
    lower = (joined - upper.astype(F32)).astype(BF)
    across = ((1,), (1,))
    both = dot(jnp.concatenate([upper, lower], axis=0), high[...], across)
    inverse = both[:count] + both[count:] + dot(upper, low[...], across)
    inverse = inverse * (1.0 / (WIDTH * math.sqrt(WIDTH)))
    for c in range(CH):
        for z in range(DEPTH):
            start = (c * DEPTH + z) * ROWS
            out[c, z] = inverse[start : start + ROWS]


def correlate(own, got, high, low, interpret=False):
    return pl.pallas_call(
        correlate_kernel,
        out_shape=jax.ShapeDtypeStruct((CH, DEPTH, ROWS, WIDTH), F32),
        name="correlate",
        interpret=interpret,
    )(own, got, high, low)


def layer_kernel(got, spread, banded, biases, projected, out, wide, first, second):
    n = MIXED * ROWS
    shape = (SPAN, TILES, n)
    flat = (SPAN * TILES, n)
    tile = iota(shape, 1).reshape(flat)
    right = iota(flat, 1) >= 64
    count = BRICK * TILES
    centre = None
    for a in range(3):
        mixed = got[:, a * PLANE : (a + 1) * PLANE, :].reshape(ROUNDS * PLANE, SPAN * TILES)
        plane = dot(mixed, spread[...], ((0,), (0,))).astype(BF)
        at = a * 256
        wide[:, at : at + 128] = plane
        plane = plane.astype(F32)
        if a == 1:
            centre = plane[TILES : TILES + count]
        upper = jnp.where(tile == 0, 0.0, pltpu.roll(plane, 1, 0))
        lower = jnp.where(tile == TILES - 1, 0.0, pltpu.roll(plane, SPAN * TILES - 1, 0))
        wide[:, at + 128 : at + 256] = jnp.where(right, upper, lower).astype(BF)
    total = biases[...]
    for b in range(3):
        total = total + dot(
            wide[b * TILES : b * TILES + count, :],
            banded[:, b * 768 : (b + 1) * 768],
            ((1,), (1,)),
        )
    hidden = jax.nn.gelu(total).astype(BF)
    mixed = dot(hidden, projected[...], ((1,), (1,)))
    done = centre + mixed
    left = iota((MIXED, 128), 1) < 64
    order = iota((256, 256), 1) == 4 * (iota((256, 256), 0) % 64) + iota((256, 256), 0) // 64
    order = order.astype(BF)
    lines = []
    for x in range(0, BRICK, 2):
        pair = done[x * TILES : (x + 2) * TILES, :].T
        y = [pair[i * MIXED : (i + 1) * MIXED, :] for i in range(ROWS)]
        lines.append(
            jnp.concatenate(
                [
                    jnp.where(left, y[0], pltpu.roll(y[1], 64, 1)),
                    jnp.where(left, y[2], pltpu.roll(y[3], 64, 1)),
                ],
                axis=1,
            )
        )
        lines.append(
            jnp.concatenate(
                [
                    jnp.where(left, pltpu.roll(y[0], 64, 1), y[1]),
                    jnp.where(left, pltpu.roll(y[2], 64, 1), y[3]),
                ],
                axis=1,
            )
        )
    ordered = dot(jnp.concatenate(lines, axis=0).astype(BF), order, ((1,), (0,)))
    for x in range(BRICK):
        rows = ordered[x * MIXED : (x + 1) * MIXED]
        first[pl.ds(x, MIXED, stride=BRICK), :] = rows[:, :128]
        second[pl.ds(x, MIXED, stride=BRICK), :] = rows[:, 128:]
    out[:, :, :128] = first[...].reshape(MIXED, BRICK, 128).astype(BF)
    out[:, :, 128:] = second[...].reshape(MIXED, BRICK, 128).astype(BF)


def layer(got, spread, banded, biases, projected, interpret=False):
    return pl.pallas_call(
        layer_kernel,
        out_shape=jax.ShapeDtypeStruct((MIXED, BRICK, TILES * ROWS), BF),
        scratch_shapes=[
            pltpu.VMEM((SPAN * TILES, 3 * 256), BF),
            pltpu.VMEM((MIXED * BRICK, 128), F32),
            pltpu.VMEM((MIXED * BRICK, 128), F32),
        ],
        name="layer",
        interpret=interpret,
    )(got, spread, banded, biases, projected)


def body(
    raw_tiles, ref_bands, shifts, matrix_ids, resample, unmix, conv_weight, conv_bias, out_weight
):
    high, low = tables()
    swap = functools.partial(lax.all_to_all, split_axis=0, concat_axis=0, tiled=True)
    spread, banded, biases, projected = prepare(
        unmix, conv_weight, conv_bias.reshape(1, -1), out_weight
    )
    high, low = jnp.asarray(high), jnp.asarray(low)
    sent, own = warp(shifts, matrix_ids, raw_tiles[0], resample)
    with jax.named_scope("tiles"):
        got = swap(sent, "tile")
    with jax.named_scope("slabs"):
        slabs = swap(regroup(got, ref_bands[0]), "round")
    correlation = correlate(own_spectra(own, high, low), slabs, high, low)
    features = layer(slabs, spread, banded, biases, projected)
    return (correlation[None], features[:, None])


def solution(mesh):
    placed = (
        P("round", None, None, "tile", None),
        P("round", "tile", None),
        P("round", "tile"),
        P("round", None),
        P(),
        P(),
        P(),
        P(),
        P(),
    )
    return jax.shard_map(
        body,
        mesh=mesh,
        in_specs=placed,
        out_specs=(P("round", None, None, "tile", None), P(None, "round", "tile", None)),
        check_vma=False,
    )
```

```python
import functools
import math

import jax
import jax.numpy as jnp
import numpy as np
from jax import lax
from jax.experimental import pallas as pl
from jax.experimental.pallas import tpu as pltpu
from jax.sharding import PartitionSpec as P

BF = jnp.bfloat16
F32 = jnp.float32
ROUNDS, TILES = 8, 64
CH, DEPTH, ROWS, WIDTH = 4, 8, 4, 512
MIXED, HIDDEN = 32, 64
HALVES, FAR = 2, 4
PAIRS = TILES // 2
PLANE = CH * ROWS
BRICK = WIDTH // TILES
SPAN = BRICK + 2
LINES = 3 * HALVES * PLANE
ALONG = SPAN * PAIRS
PADDED = 384


def device(half, far, pair, core):
    return (half * FAR + far) * TILES + 2 * pair + core


RINGS = [
    [device(half, far, pair, core) for half in range(HALVES) for pair in range(PAIRS)]
    for far in range(FAR)
    for core in range(2)
]
NEAR = [
    [device(half, far, pair, core) for far in range(FAR) for core in range(2)]
    for half in range(HALVES)
    for pair in range(PAIRS)
]


def iota(shape, dim):
    return lax.broadcasted_iota(jnp.int32, shape, dim)


def dot(a, b, dims):
    return lax.dot_general(a, b, (dims, ((), ())), preferred_element_type=F32)


def warp_kernel(shift, ids, raw, table, out, own, mats, sems):
    copies = [
        pltpu.make_async_copy(table.at[ids[0, c]], mats.at[c], sems.at[c]) for c in range(CH)
    ]
    for copy in copies:
        copy.start()
    by = shift[0, 0]
    warped = []
    for c in range(CH):
        rows = jnp.concatenate([raw[c, z].astype(F32) for z in range(DEPTH)], axis=0)
        rows = pltpu.roll(rows, by, 1).astype(BF)
        copies[c].wait()
        result = dot(rows, mats[c], ((1,), (0,)))
        own[c] = result.astype(BF)
        warped.append(result.reshape(DEPTH // 2, 2 * ROWS, WIDTH))
    low = iota((DEPTH // 2, 2 * ROWS, WIDTH), 1) < ROWS
    even, odd = [], []
    for c in range(0, CH, 2):
        a, b = warped[c], warped[c + 1]
        even.append(jnp.where(low, a, pltpu.roll(b, ROWS, 1)))
        odd.append(jnp.where(low, pltpu.roll(a, ROWS, 1), b))
    planes = []
    for z in range(DEPTH):
        planes += [p[z // 2] for p in (odd if z % 2 else even)]
    upright = jnp.concatenate(planes, axis=0).T.reshape(PAIRS, 2, BRICK, DEPTH * PLANE)
    left, right = upright[:, 0], upright[:, 1]
    edge = jnp.zeros((1, BRICK, DEPTH * PLANE), F32)
    before = jnp.concatenate([edge, right[:-1]], axis=0)
    after = jnp.concatenate([left[1:], edge], axis=0)
    row, lane = iota(left.shape, 1), iota(left.shape, 2)

    def put(base, value, start, to, width, only=None, turn=0):
        value = pltpu.roll(value, turn, 1) if turn else value
        value = pltpu.roll(value, (to - start) % 128, 2) if to != start else value
        here = (lane >= to) & (lane < to + width)
        return jnp.where(here if only is None else here & (row == only), value, base)

    for half in range(HALVES):
        start = 64 * half
        main = put(left, right, start, 64, 64) if half == 0 else put(right, left, start, 0, 64)
        more = jnp.zeros(left.shape, F32)
        more = put(more, before, start, 64, 64, 0, 1)
        more = put(more, after, start, 64, 64, 1, 1)
        outer = 64 if half == 0 else 48
        slot = 32 if half == 0 else 0
        more = put(more, left, outer, slot, PLANE)
        more = put(more, right, outer, slot + PLANE, PLANE)
        more = put(more, before, outer, 64 + slot // 2, PLANE, 2, 3)
        more = put(more, after, outer, 96 + slot // 2, PLANE, 2, 2)
        out[half * PAIRS : (half + 1) * PAIRS] = jnp.concatenate([main, more], axis=1).astype(BF)


def warp(shift, ids, raw, table, interpret=False):
    return pl.pallas_call(
        warp_kernel,
        out_shape=(
            pltpu.VMEM((TILES, 2 * BRICK, DEPTH * PLANE), BF),
            pltpu.VMEM((CH, DEPTH * ROWS, WIDTH), BF),
        ),
        in_specs=[
            pl.BlockSpec(memory_space=pltpu.SMEM),
            pl.BlockSpec(memory_space=pltpu.SMEM),
            pl.BlockSpec(memory_space=pltpu.VMEM),
            pl.BlockSpec(memory_space=pl.ANY),
        ],
        scratch_shapes=[
            pltpu.VMEM((CH, WIDTH, WIDTH), BF),
            pltpu.SemaphoreType.DMA((CH,)),
        ],
        name="warp",
        interpret=interpret,
    )(shift, ids, raw, table)


def prepare_kernel(unmix, conv, bias, project, spread, banded, biases, projected):
    n = MIXED * ROWS
    k = iota((n, MIXED), 0)
    source = (k // PLANE % HALVES * FAR + k // (HALVES * PLANE)) * CH + k // ROWS % CH
    pick_in = (source == iota((n, MIXED), 1)).astype(BF)
    pick_out = (iota((MIXED, n), 1) % MIXED == iota((MIXED, n), 0)).astype(BF)
    tall = dot(pick_in, unmix[...], ((1,), (1,))).astype(BF)
    wide = dot(tall, pick_out, ((1,), (0,)))
    own = iota((n, n), 0) % ROWS == iota((n, n), 1) // MIXED
    spread[...] = jnp.where(own, wide, 0.0).astype(BF)
    gap = jnp.zeros((HIDDEN, MIXED), BF)
    for ab in range(9):
        at = (ab % 3 * 3 + ab // 3) * 256
        d = [conv[3 * ab + i] for i in range(3)]
        rows = [
            [d[1], d[2], gap, gap, gap, gap, gap, d[0]],
            [d[0], d[1], d[2], gap, gap, gap, gap, gap],
            [gap, d[0], d[1], d[2], gap, gap, gap, gap],
            [gap, gap, d[0], d[1], d[2], gap, gap, gap],
        ]
        for y in range(ROWS):
            banded[y * HIDDEN : (y + 1) * HIDDEN, at : at + 256] = jnp.concatenate(
                rows[y], axis=1
            )
    biases[...] = jnp.concatenate([bias[...]] * ROWS, axis=1)
    hole = jnp.zeros((MIXED, HIDDEN), BF)
    for y in range(ROWS):
        row = [project[...] if i == y else hole for i in range(ROWS)]
        projected[y * MIXED : (y + 1) * MIXED, :] = jnp.concatenate(row, axis=1)


def prepare(unmix, conv, bias, project, interpret=False):
    return pl.pallas_call(
        prepare_kernel,
        out_shape=(
            pltpu.VMEM((MIXED * ROWS, MIXED * ROWS), BF),
            jax.ShapeDtypeStruct((HIDDEN * ROWS, 9 * 256), BF),
            pltpu.VMEM((1, HIDDEN * ROWS), F32),
            pltpu.VMEM((MIXED * ROWS, HIDDEN * ROWS), BF),
        ),
        name="prepare",
        interpret=interpret,
    )(unmix, conv, bias, project)


def regroup_kernel(got, band, other, out, tall):
    tall[...] = got[...].astype(F32).reshape(TILES * 2 * BRICK, DEPTH * PLANE)
    turned = []
    for q in range(BRICK):
        both = [tall[pl.ds(q + at, TILES, stride=2 * BRICK), :] for at in (0, BRICK)]
        turned.append(jnp.concatenate(both, axis=0).T)

    def piece(slot, column):
        x = column - 1
        if 0 <= x < 2 * BRICK:
            block, q = x // BRICK, x % BRICK
            if 1 <= slot <= 4:
                start, at = block * 64 + (slot - 1) * PLANE, 0
            else:
                start, at = (32 if slot else 0) + block * PLANE, 64
        else:
            side = 0 if x < 0 else 1
            if 1 <= slot <= 4:
                q, start, at = side, 64 + (slot - 1) * PLANE, 64
            else:
                q, start, at = 2, 64 + 32 * side + (PLANE if slot else 0), 64
        return turned[q][start : start + PLANE], at

    refs = jnp.concatenate([band[...].astype(F32), other[...].astype(F32)], axis=0)
    marks = []
    for p in range(0, 8, 2):
        pair = refs[:, p * 64 : (p + 2) * 64]
        marks.append(jnp.concatenate([pltpu.roll(pair, 64, 1), pair], axis=0))
    lane = iota((PLANE, 128), 1)
    for core in range(2):
        for slot in range(6):
            pieces = [piece(slot, core * BRICK + k) for k in range(SPAN)]
            for half in range(HALVES):
                blocks = []
                for m in range(3):
                    block = jnp.zeros((PLANE, 128), F32)
                    for k in range(4 * m, min(4 * m + 4, SPAN)):
                        rows, at = pieces[k]
                        to = k % 4 * PAIRS
                        turn = (to - at - half * PAIRS) % 128
                        rows = pltpu.roll(rows, turn, 1) if turn else rows
                        block = jnp.where((lane >= to) & (lane < to + PAIRS), rows, block)
                    blocks.append(block)
                main = [block.astype(BF) for block in blocks[:2]]
                for far in range(FAR):
                    step = slot - far
                    if not 0 <= step < 3:
                        continue
                    w = step * HALVES + half
                    last = jnp.where(lane >= 64, marks[w], blocks[2]) if w < 4 else blocks[2]
                    rows = slice(w * PLANE, (w + 1) * PLANE)
                    out[2 * far + core, rows, :128] = main[0]
                    out[2 * far + core, rows, 128:256] = main[1]
                    out[2 * far + core, rows, 256:] = last.astype(BF)


def regroup(got, band, other, interpret=False):
    return pl.pallas_call(
        regroup_kernel,
        out_shape=pltpu.VMEM((2 * FAR, LINES, PADDED), BF),
        scratch_shapes=[pltpu.VMEM((TILES * 2 * BRICK, DEPTH * PLANE), F32)],
        name="regroup",
        interpret=interpret,
    )(got, band, other)


def tables():
    x = np.arange(WIDTH, dtype=np.int64)
    half = WIDTH // 2
    frequency = np.where(x < half, x, np.where(x == half, half, x - half))
    angles = (x[:, None] * frequency[None, :] % WIDTH) * (2.0 * math.pi / WIDTH)
    table = np.where((x <= half)[None, :], np.cos(angles), np.sin(angles)).astype(np.float32)
    high = table.astype(jnp.bfloat16)
    low = (table - high.astype(np.float32)).astype(jnp.bfloat16)
    return high, low


def spectra_kernel(own, high, low, out):
    rows = own[...].reshape(CH * DEPTH * ROWS, WIDTH)
    out[...] = dot(rows, high[...], ((1,), (0,))) + dot(rows, low[...], ((1,), (0,)))


def own_spectra(own, high, low, interpret=False):
    return pl.pallas_call(
        spectra_kernel,
        out_shape=pltpu.VMEM((CH * DEPTH * ROWS, WIDTH), F32),
        name="spectra",
        interpret=interpret,
    )(own, high, low)


def correlate_kernel(place, own, got, high, low, out):
    half = WIDTH // 2
    count = CH * DEPTH * ROWS
    left = iota((2 * ROWS, 128), 1) < 64
    near, away = [], []
    for far in range(FAR):
        pieces = jnp.where(
            place[1] == 0, got[2 * far].astype(F32), got[2 * far + 1].astype(F32)
        )
        lanes = []
        for p in range(0, 8, 2):
            a = pieces[p * 2 * ROWS : (p + 1) * 2 * ROWS]
            b = pieces[(p + 1) * 2 * ROWS : (p + 2) * 2 * ROWS]
            lanes.append(jnp.where(left, pltpu.roll(a, 64, 1), b))
        rows = jnp.concatenate(lanes, axis=1)
        near.append(rows[:ROWS])
        away.append(rows[ROWS:])
    near, away = jnp.concatenate(near, axis=0), jnp.concatenate(away, axis=0)
    first_half = place[0] == 0
    band = jnp.concatenate(
        [jnp.where(first_half, near, away), jnp.where(first_half, away, near)], axis=0
    ).astype(BF)
    along = ((1,), (0,))
    band = dot(band, high[...], along) + dot(band, low[...], along)
    own_cos = own[:, :half].reshape(CH, DEPTH * ROWS, half)
    own_sin = own[:, half:].reshape(CH, DEPTH * ROWS, half)
    band_cos = band[:, :half]
    band_sin = band[:, half:]
    first = iota(own_cos.shape, 2) == 0
    sines = own_sin * band_sin
    cosines = own_cos * band_cos
    real = jnp.where(first, cosines, 2.0 * (cosines + sines))
    imag = jnp.where(first, sines, 2.0 * (own_sin * band_cos - own_cos * band_sin))
    joined = jnp.concatenate([real.reshape(count, half), imag.reshape(count, half)], axis=1)
    upper = joined.astype(BF)
    lower = (joined - upper.astype(F32)).astype(BF)
    across = ((1,), (1,))
    both = dot(jnp.concatenate([upper, lower], axis=0), high[...], across)
    inverse = both[:count] + both[count:] + dot(upper, low[...], across)
    inverse = inverse * (1.0 / (WIDTH * math.sqrt(WIDTH)))
    for c in range(CH):
        for z in range(DEPTH):
            start = (c * DEPTH + z) * ROWS
            out[c, z] = inverse[start : start + ROWS]


def correlate(place, own, got, high, low, interpret=False):
    def whole(*shape):
        return pl.BlockSpec(shape, lambda i: (0,) * len(shape))

    return pl.pallas_call(
        correlate_kernel,
        grid=(1,),
        in_specs=[
            pl.BlockSpec(memory_space=pltpu.SMEM),
            whole(*own.shape),
            pl.BlockSpec((2 * FAR, 64, 128), lambda i: (0, 0, 2)),
            whole(WIDTH, WIDTH),
            whole(WIDTH, WIDTH),
        ],
        out_specs=whole(CH, DEPTH, ROWS, WIDTH),
        out_shape=jax.ShapeDtypeStruct((CH, DEPTH, ROWS, WIDTH), F32),
        name="correlate",
        interpret=interpret,
    )(place, own, got, high, low)


def layer_kernel(got, spread, banded, biases, projected, out, wide, first, second, weights, sem):
    fetch = pltpu.make_async_copy(banded, weights, sem.at[0])
    fetch.start()
    n = MIXED * ROWS
    pair = iota((SPAN, PAIRS, n), 1).reshape(ALONG, n)
    right = iota((ALONG, n), 1) >= 64
    count = BRICK * PAIRS
    centre = None
    for a in range(3):
        at = a * 256
        planes = []
        for core in range(2):
            mixed = jnp.concatenate(
                [
                    got[2 * far + core, a * HALVES * PLANE : (a + 1) * HALVES * PLANE, :]
                    for far in range(FAR)
                ],
                axis=0,
            )
            plane = dot(mixed, spread[...], ((0,), (0,)))[:ALONG].astype(BF)
            wide[core, :, at : at + 128] = plane
            planes.append(plane.astype(F32))
        even, odd = planes
        if a == 1:
            centre = jnp.concatenate([p[PAIRS : PAIRS + count] for p in planes], axis=0)
        upper = jnp.where(pair == 0, 0.0, pltpu.roll(odd, 1, 0))
        lower = jnp.where(pair == PAIRS - 1, 0.0, pltpu.roll(even, ALONG - 1, 0))
        wide[0, :, at + 128 : at + 256] = jnp.where(right, upper, odd).astype(BF)
        wide[1, :, at + 128 : at + 256] = jnp.where(right, even, lower).astype(BF)
    fetch.wait()
    total = biases[...]
    for b in range(3):
        rows = jnp.concatenate(
            [wide[core, b * PAIRS : b * PAIRS + count, :] for core in range(2)], axis=0
        )
        total = total + dot(rows, weights[:, b * 768 : (b + 1) * 768], ((1,), (1,)))
    hidden = jax.nn.gelu(total).astype(BF)
    mixed = dot(hidden, projected[...], ((1,), (1,)))
    done = centre + mixed
    left = iota((MIXED, 128), 1) < 64
    k = iota((256, 256), 0)
    order = iota((256, 256), 1) == 8 * (k % PAIRS) + 4 * (k // PAIRS % 2) + k // 64
    order = order.astype(BF)
    lines = []
    for x in range(0, BRICK, 2):
        pair = jnp.concatenate(
            [
                done[core * count + at * PAIRS : core * count + (at + 1) * PAIRS]
                for at in (x, x + 1)
                for core in range(2)
            ],
            axis=0,
        ).T
        y = [pair[i * MIXED : (i + 1) * MIXED, :] for i in range(ROWS)]
        lines.append(
            jnp.concatenate(
                [
                    jnp.where(left, y[0], pltpu.roll(y[1], 64, 1)),
                    jnp.where(left, y[2], pltpu.roll(y[3], 64, 1)),
                ],
                axis=1,
            )
        )
        lines.append(
            jnp.concatenate(
                [
                    jnp.where(left, pltpu.roll(y[0], 64, 1), y[1]),
                    jnp.where(left, pltpu.roll(y[2], 64, 1), y[3]),
                ],
                axis=1,
            )
        )
    ordered = dot(jnp.concatenate(lines, axis=0).astype(BF), order, ((1,), (0,)))
    for x in range(BRICK):
        rows = ordered[x * MIXED : (x + 1) * MIXED]
        first[pl.ds(x, MIXED, stride=BRICK), :] = rows[:, :128]
        second[pl.ds(x, MIXED, stride=BRICK), :] = rows[:, 128:]
    out[:, :, :128] = first[...].reshape(MIXED, BRICK, 128).astype(BF)
    out[:, :, 128:] = second[...].reshape(MIXED, BRICK, 128).astype(BF)


def layer(got, spread, banded, biases, projected, interpret=False):
    inside = pl.BlockSpec(memory_space=pltpu.VMEM)
    return pl.pallas_call(
        layer_kernel,
        in_specs=[inside, inside, pl.BlockSpec(memory_space=pl.ANY), inside, inside],
        out_shape=jax.ShapeDtypeStruct((MIXED, BRICK, TILES * ROWS), BF),
        scratch_shapes=[
            pltpu.VMEM((2, ALONG, 3 * 256), BF),
            pltpu.VMEM((MIXED * BRICK, 128), F32),
            pltpu.VMEM((MIXED * BRICK, 128), F32),
            pltpu.VMEM((HIDDEN * ROWS, 9 * 256), BF),
            pltpu.SemaphoreType.DMA((1,)),
        ],
        name="layer",
        interpret=interpret,
    )(got, spread, banded, biases, projected)


def close(value):
    return pltpu.with_memory_space_constraint(value, pltpu.VMEM)


def body(
    raw_tiles, ref_bands, shifts, matrix_ids, resample, unmix, conv_weight, conv_bias, out_weight
):
    high, low = tables()
    swap = functools.partial(
        lax.all_to_all, axis_name=("round", "tile"), split_axis=0, concat_axis=0, tiled=True
    )
    place = jnp.stack([lax.axis_index("round") >> 2, lax.axis_index("tile") & 1])
    band = ref_bands[0]
    other = lax.ppermute(band, "round", [(i, (i + FAR) % ROUNDS) for i in range(ROUNDS)])
    spread, banded, biases, projected = prepare(
        unmix, conv_weight, conv_bias.reshape(1, -1), out_weight
    )
    spread, biases, projected = map(close, (spread, biases, projected))
    high, low = close(jnp.asarray(high)), close(jnp.asarray(low))
    sent, own = map(close, warp(shifts, matrix_ids, raw_tiles[0], resample))
    got = close(swap(sent, axis_index_groups=RINGS))
    slabs = close(swap(close(regroup(got, band, other)), axis_index_groups=NEAR))
    spectra = close(own_spectra(own, high, low))
    correlation = correlate(place, spectra, slabs, high, low)
    features = layer(slabs, spread, banded, biases, projected)
    return (correlation[None], features[:, None])


def solution(mesh):
    placed = (
        P("round", None, None, "tile", None),
        P("round", "tile", None),
        P("round", "tile"),
        P("round", None),
        P(),
        P(),
        P(),
        P(),
        P(),
    )
    return jax.shard_map(
        body,
        mesh=mesh,
        in_specs=placed,
        out_specs=(P("round", None, None, "tile", None), P(None, "round", "tile", None)),
        check_vma=False,
    )
```

```python
import functools
import math

import jax
import jax.numpy as jnp
import numpy as np
from jax import lax
from jax.experimental import pallas as pl
from jax.experimental.pallas import tpu as pltpu
from jax.sharding import PartitionSpec as P

BF = jnp.bfloat16
F32 = jnp.float32
ROUNDS, TILES = 8, 64
CH, DEPTH, ROWS, WIDTH = 4, 8, 4, 512
MIXED, HIDDEN = 32, 64
HALVES, FAR = 2, 4
PAIRS = TILES // 2
PLANE = CH * ROWS
BRICK = WIDTH // TILES
SPAN = BRICK + 2
LINES = 3 * HALVES * PLANE
ALONG = SPAN * PAIRS
PADDED = 384


def device(half, far, pair, core):
    return (half * FAR + far) * TILES + 2 * pair + core


RINGS = [
    [device(half, far, pair, core) for half in range(HALVES) for pair in range(PAIRS)]
    for far in range(FAR)
    for core in range(2)
]
NEAR = [
    [device(half, far, pair, core) for far in range(FAR) for core in range(2)]
    for half in range(HALVES)
    for pair in range(PAIRS)
]


def iota(shape, dim):
    return lax.broadcasted_iota(jnp.int32, shape, dim)


def dot(a, b, dims):
    return lax.dot_general(a, b, (dims, ((), ())), preferred_element_type=F32)


def warp_kernel(shift, ids, tiles, table, out, own, raw, mats, chosen, sent, sems):
    inward = [
        pltpu.make_async_copy(tiles, raw, sems.at[0]),
        pltpu.make_async_copy(ids, chosen, sems.at[1]),
    ]
    inward += [
        pltpu.make_async_copy(table.at[k], mats.at[k], sems.at[2 + k]) for k in range(len(mats))
    ]
    for copy in inward:
        copy.start()
    by = shift[0, 0]
    inward[0].wait()
    turned = []
    for c in range(CH):
        rows = jnp.concatenate([raw[c, z].astype(F32) for z in range(DEPTH)], axis=0)
        turned.append(pltpu.roll(rows, by, 1).astype(BF))
    for copy in inward[1:]:
        copy.wait()
    warped = []
    for c in range(CH):
        result = dot(turned[c], mats[chosen[0, c]], ((1,), (0,)))
        own[c] = result.astype(BF)
        warped.append(result.reshape(DEPTH // 2, 2 * ROWS, WIDTH))
    low = iota((DEPTH // 2, 2 * ROWS, WIDTH), 1) < ROWS
    even, odd = [], []
    for c in range(0, CH, 2):
        a, b = warped[c], warped[c + 1]
        even.append(jnp.where(low, a, pltpu.roll(b, ROWS, 1)))
        odd.append(jnp.where(low, pltpu.roll(a, ROWS, 1), b))
    planes = []
    for z in range(DEPTH):
        planes += [p[z // 2] for p in (odd if z % 2 else even)]
    upright = jnp.concatenate(planes, axis=0).T.reshape(PAIRS, 2, BRICK, DEPTH * PLANE)
    left, right = upright[:, 0], upright[:, 1]
    edge = jnp.zeros((1, BRICK, DEPTH * PLANE), F32)
    before = jnp.concatenate([edge, right[:-1]], axis=0)
    after = jnp.concatenate([left[1:], edge], axis=0)
    row, lane = iota(left.shape, 1), iota(left.shape, 2)

    def put(base, value, start, to, width, only=None, turn=0):
        value = pltpu.roll(value, turn, 1) if turn else value
        value = pltpu.roll(value, (to - start) % 128, 2) if to != start else value
        here = (lane >= to) & (lane < to + width)
        return jnp.where(here if only is None else here & (row == only), value, base)

    outward = []
    for half in range(HALVES):
        start = 64 * half
        main = put(left, right, start, 64, 64) if half == 0 else put(right, left, start, 0, 64)
        more = jnp.zeros(left.shape, F32)
        more = put(more, before, start, 64, 64, 0, 1)
        more = put(more, after, start, 64, 64, 1, 1)
        outer = 64 if half == 0 else 48
        slot = 32 if half == 0 else 0
        more = put(more, left, outer, slot, PLANE)
        more = put(more, right, outer, slot + PLANE, PLANE)
        more = put(more, before, outer, 64 + slot // 2, PLANE, 2, 3)
        more = put(more, after, outer, 96 + slot // 2, PLANE, 2, 2)
        part = slice(half * PAIRS, (half + 1) * PAIRS)
        sent[part] = jnp.concatenate([main, more], axis=1).astype(BF)
        copy = pltpu.make_async_copy(sent.at[part], out.at[part], sems.at[6 + half])
        copy.start()
        outward.append(copy)
    for copy in outward:
        copy.wait()


def warp(shift, ids, raw, table, interpret=False):
    away = pl.BlockSpec(memory_space=pl.ANY)
    shape = (TILES, 2 * BRICK, DEPTH * PLANE)
    return pl.pallas_call(
        warp_kernel,
        out_shape=(
            jax.ShapeDtypeStruct(shape, BF),
            pltpu.VMEM((CH, DEPTH * ROWS, WIDTH), BF),
        ),
        in_specs=[pl.BlockSpec(memory_space=pltpu.SMEM), away, away, away],
        out_specs=(away, pl.BlockSpec(memory_space=pltpu.VMEM)),
        scratch_shapes=[
            pltpu.VMEM(raw.shape, BF),
            pltpu.VMEM(table.shape, BF),
            pltpu.SMEM(ids.shape, jnp.int32),
            pltpu.VMEM(shape, BF),
            pltpu.SemaphoreType.DMA((8,)),
        ],
        name="warp",
        interpret=interpret,
    )(shift, ids, raw, table)


def prepare_kernel(unmix, conv, bias, project, spread, banded, biases, projected):
    n = MIXED * ROWS
    k = iota((n, MIXED), 0)
    source = (k // PLANE % HALVES * FAR + k // (HALVES * PLANE)) * CH + k // ROWS % CH
    pick_in = (source == iota((n, MIXED), 1)).astype(BF)
    pick_out = (iota((MIXED, n), 1) % MIXED == iota((MIXED, n), 0)).astype(BF)
    tall = dot(pick_in, unmix[...], ((1,), (1,))).astype(BF)
    wide = dot(tall, pick_out, ((1,), (0,)))
    own = iota((n, n), 0) % ROWS == iota((n, n), 1) // MIXED
    spread[...] = jnp.where(own, wide, 0.0).astype(BF)
    gap = jnp.zeros((HIDDEN, MIXED), BF)
    for ab in range(9):
        at = (ab % 3 * 3 + ab // 3) * 256
        d = [conv[3 * ab + i] for i in range(3)]
        rows = [
            [d[1], d[2], gap, gap, gap, gap, gap, d[0]],
            [d[0], d[1], d[2], gap, gap, gap, gap, gap],
            [gap, d[0], d[1], d[2], gap, gap, gap, gap],
            [gap, gap, d[0], d[1], d[2], gap, gap, gap],
        ]
        for y in range(ROWS):
            banded[y * HIDDEN : (y + 1) * HIDDEN, at : at + 256] = jnp.concatenate(
                rows[y], axis=1
            )
    biases[...] = jnp.concatenate([bias[...]] * ROWS, axis=1)
    hole = jnp.zeros((MIXED, HIDDEN), BF)
    for y in range(ROWS):
        row = [project[...] if i == y else hole for i in range(ROWS)]
        projected[y * MIXED : (y + 1) * MIXED, :] = jnp.concatenate(row, axis=1)


def prepare(unmix, conv, bias, project, interpret=False):
    return pl.pallas_call(
        prepare_kernel,
        out_shape=(
            pltpu.VMEM((MIXED * ROWS, MIXED * ROWS), BF),
            jax.ShapeDtypeStruct((HIDDEN * ROWS, 9 * 256), BF),
            pltpu.VMEM((1, HIDDEN * ROWS), F32),
            pltpu.VMEM((MIXED * ROWS, HIDDEN * ROWS), BF),
        ),
        name="prepare",
        interpret=interpret,
    )(unmix, conv, bias, project)


def regroup_kernel(got, band, other, out, tall, sent, sems):
    tall[...] = got[...].astype(F32).reshape(TILES * 2 * BRICK, DEPTH * PLANE)
    turned = []
    for q in range(BRICK):
        both = [tall[pl.ds(q + at, TILES, stride=2 * BRICK), :] for at in (0, BRICK)]
        turned.append(jnp.concatenate(both, axis=0).T)

    def piece(slot, column):
        x = column - 1
        if 0 <= x < 2 * BRICK:
            block, q = x // BRICK, x % BRICK
            if 1 <= slot <= 4:
                start, at = block * 64 + (slot - 1) * PLANE, 0
            else:
                start, at = (32 if slot else 0) + block * PLANE, 64
        else:
            side = 0 if x < 0 else 1
            if 1 <= slot <= 4:
                q, start, at = side, 64 + (slot - 1) * PLANE, 64
            else:
                q, start, at = 2, 64 + 32 * side + (PLANE if slot else 0), 64
        return turned[q][start : start + PLANE], at

    refs = jnp.concatenate([band[...].astype(F32), other[...].astype(F32)], axis=0)
    marks = []
    for p in range(0, 8, 2):
        pair = refs[:, p * 64 : (p + 2) * 64]
        marks.append(jnp.concatenate([pltpu.roll(pair, 64, 1), pair], axis=0))
    lane = iota((PLANE, 128), 1)
    outward = []
    for core in range(2):
        for slot in range(6):
            pieces = [piece(slot, core * BRICK + k) for k in range(SPAN)]
            for half in range(HALVES):
                blocks = []
                for m in range(3):
                    block = jnp.zeros((PLANE, 128), F32)
                    for k in range(4 * m, min(4 * m + 4, SPAN)):
                        rows, at = pieces[k]
                        to = k % 4 * PAIRS
                        turn = (to - at - half * PAIRS) % 128
                        rows = pltpu.roll(rows, turn, 1) if turn else rows
                        block = jnp.where((lane >= to) & (lane < to + PAIRS), rows, block)
                    blocks.append(block)
                main = [block.astype(BF) for block in blocks[:2]]
                for far in range(FAR):
                    step = slot - far
                    if not 0 <= step < 3:
                        continue
                    w = step * HALVES + half
                    last = jnp.where(lane >= 64, marks[w], blocks[2]) if w < 4 else blocks[2]
                    rows = slice(w * PLANE, (w + 1) * PLANE)
                    sent[2 * far + core, rows, :128] = main[0]
                    sent[2 * far + core, rows, 128:256] = main[1]
                    sent[2 * far + core, rows, 256:] = last.astype(BF)
            if slot >= 2:
                peer = 2 * (slot - 2) + core
                copy = pltpu.make_async_copy(sent.at[peer], out.at[peer], sems.at[peer])
                copy.start()
                outward.append(copy)
    for copy in outward:
        copy.wait()


def regroup(got, band, other, interpret=False):
    shape = (2 * FAR, LINES, PADDED)
    return pl.pallas_call(
        regroup_kernel,
        out_shape=jax.ShapeDtypeStruct(shape, BF),
        in_specs=[pl.BlockSpec(memory_space=pltpu.VMEM)] * 3,
        out_specs=pl.BlockSpec(memory_space=pl.ANY),
        scratch_shapes=[
            pltpu.VMEM((TILES * 2 * BRICK, DEPTH * PLANE), F32),
            pltpu.VMEM(shape, BF),
            pltpu.SemaphoreType.DMA((2 * FAR,)),
        ],
        name="regroup",
        interpret=interpret,
    )(got, band, other)


def tables():
    x = np.arange(WIDTH, dtype=np.int64)
    half = WIDTH // 2
    frequency = np.where(x < half, x, np.where(x == half, half, x - half))
    angles = (x[:, None] * frequency[None, :] % WIDTH) * (2.0 * math.pi / WIDTH)
    table = np.where((x <= half)[None, :], np.cos(angles), np.sin(angles)).astype(np.float32)
    high = table.astype(jnp.bfloat16)
    low = (table - high.astype(np.float32)).astype(jnp.bfloat16)
    return high, low


def spectra_kernel(own, high, low, out):
    rows = own[...].reshape(CH * DEPTH * ROWS, WIDTH)
    out[...] = dot(rows, high[...], ((1,), (0,))) + dot(rows, low[...], ((1,), (0,)))


def own_spectra(own, high, low, interpret=False):
    return pl.pallas_call(
        spectra_kernel,
        out_shape=pltpu.VMEM((CH * DEPTH * ROWS, WIDTH), F32),
        name="spectra",
        interpret=interpret,
    )(own, high, low)


def correlate(place, own, got, high, low, out):
    half = WIDTH // 2
    count = CH * DEPTH * ROWS
    left = iota((2 * ROWS, 128), 1) < 64
    near, away = [], []
    for far in range(FAR):
        pieces = jnp.where(
            place[1, :1, :128] == 0,
            got[2 * far, :64, 256:].astype(F32),
            got[2 * far + 1, :64, 256:].astype(F32),
        )
        lanes = []
        for p in range(0, 8, 2):
            a = pieces[p * 2 * ROWS : (p + 1) * 2 * ROWS]
            b = pieces[(p + 1) * 2 * ROWS : (p + 2) * 2 * ROWS]
            lanes.append(jnp.where(left, pltpu.roll(a, 64, 1), b))
        rows = jnp.concatenate(lanes, axis=1)
        near.append(rows[:ROWS])
        away.append(rows[ROWS:])
    near, away = jnp.concatenate(near, axis=0), jnp.concatenate(away, axis=0)
    first_half = place[0, :1, :] == 0
    band = jnp.concatenate(
        [jnp.where(first_half, near, away), jnp.where(first_half, away, near)], axis=0
    ).astype(BF)
    along = ((1,), (0,))
    band = dot(band, high[...], along) + dot(band, low[...], along)
    own_cos = own[:, :half].reshape(CH, DEPTH * ROWS, half)
    own_sin = own[:, half:].reshape(CH, DEPTH * ROWS, half)
    band_cos = band[:, :half]
    band_sin = band[:, half:]
    first = iota(own_cos.shape, 2) == 0
    sines = own_sin * band_sin
    cosines = own_cos * band_cos
    real = jnp.where(first, cosines, 2.0 * (cosines + sines))
    imag = jnp.where(first, sines, 2.0 * (own_sin * band_cos - own_cos * band_sin))
    joined = jnp.concatenate([real.reshape(count, half), imag.reshape(count, half)], axis=1)
    upper = joined.astype(BF)
    lower = (joined - upper.astype(F32)).astype(BF)
    across = ((1,), (1,))
    both = dot(jnp.concatenate([upper, lower], axis=0), high[...], across)
    inverse = both[:count] + both[count:] + dot(upper, low[...], across)
    inverse = inverse * (1.0 / (WIDTH * math.sqrt(WIDTH)))
    for c in range(CH):
        for z in range(DEPTH):
            start = (c * DEPTH + z) * ROWS
            out[c, z] = inverse[start : start + ROWS]


def finish_kernel(
    place, own, got, high, low, spread, banded, biases, projected, away, out,
    found, wide, first, second, weights, sems,
):
    fetch = pltpu.make_async_copy(banded, weights, sems.at[0])
    fetch.start()
    correlate(place, own, got, high, low, found)
    leave = pltpu.make_async_copy(found, away, sems.at[1])
    leave.start()
    n = MIXED * ROWS
    pair = iota((SPAN, PAIRS, n), 1).reshape(ALONG, n)
    right = iota((ALONG, n), 1) >= 64
    count = BRICK * PAIRS
    centre = None
    for a in range(3):
        at = a * 256
        planes = []
        for core in range(2):
            mixed = jnp.concatenate(
                [
                    got[2 * far + core, a * HALVES * PLANE : (a + 1) * HALVES * PLANE, :]
                    for far in range(FAR)
                ],
                axis=0,
            )
            plane = dot(mixed, spread[...], ((0,), (0,)))[:ALONG].astype(BF)
            wide[core, :, at : at + 128] = plane
            planes.append(plane.astype(F32))
        even, odd = planes
        if a == 1:
            centre = jnp.concatenate([p[PAIRS : PAIRS + count] for p in planes], axis=0)
        upper = jnp.where(pair == 0, 0.0, pltpu.roll(odd, 1, 0))
        lower = jnp.where(pair == PAIRS - 1, 0.0, pltpu.roll(even, ALONG - 1, 0))
        wide[0, :, at + 128 : at + 256] = jnp.where(right, upper, odd).astype(BF)
        wide[1, :, at + 128 : at + 256] = jnp.where(right, even, lower).astype(BF)
    fetch.wait()
    total = biases[...]
    for b in range(3):
        rows = jnp.concatenate(
            [wide[core, b * PAIRS : b * PAIRS + count, :] for core in range(2)], axis=0
        )
        total = total + dot(rows, weights[:, b * 768 : (b + 1) * 768], ((1,), (1,)))
    hidden = jax.nn.gelu(total).astype(BF)
    mixed = dot(hidden, projected[...], ((1,), (1,)))
    done = centre + mixed
    left = iota((MIXED, 128), 1) < 64
    k = iota((256, 256), 0)
    order = iota((256, 256), 1) == 8 * (k % PAIRS) + 4 * (k // PAIRS % 2) + k // 64
    order = order.astype(BF)
    lines = []
    for x in range(0, BRICK, 2):
        pair = jnp.concatenate(
            [
                done[core * count + at * PAIRS : core * count + (at + 1) * PAIRS]
                for at in (x, x + 1)
                for core in range(2)
            ],
            axis=0,
        ).T
        y = [pair[i * MIXED : (i + 1) * MIXED, :] for i in range(ROWS)]
        lines.append(
            jnp.concatenate(
                [
                    jnp.where(left, y[0], pltpu.roll(y[1], 64, 1)),
                    jnp.where(left, y[2], pltpu.roll(y[3], 64, 1)),
                ],
                axis=1,
            )
        )
        lines.append(
            jnp.concatenate(
                [
                    jnp.where(left, pltpu.roll(y[0], 64, 1), y[1]),
                    jnp.where(left, pltpu.roll(y[2], 64, 1), y[3]),
                ],
                axis=1,
            )
        )
    ordered = dot(jnp.concatenate(lines, axis=0).astype(BF), order, ((1,), (0,)))
    for x in range(BRICK):
        rows = ordered[x * MIXED : (x + 1) * MIXED]
        first[pl.ds(x, MIXED, stride=BRICK), :] = rows[:, :128]
        second[pl.ds(x, MIXED, stride=BRICK), :] = rows[:, 128:]
    out[:, :, :128] = first[...].reshape(MIXED, BRICK, 128).astype(BF)
    out[:, :, 128:] = second[...].reshape(MIXED, BRICK, 128).astype(BF)
    leave.wait()


def finish(place, own, got, high, low, spread, banded, biases, projected, interpret=False):
    inside = pl.BlockSpec(memory_space=pltpu.VMEM)
    outside = pl.BlockSpec(memory_space=pl.ANY)
    found = (CH, DEPTH, ROWS, WIDTH)
    return pl.pallas_call(
        finish_kernel,
        in_specs=[inside] * 6 + [outside] + [inside] * 2,
        out_specs=(outside, inside),
        out_shape=(
            jax.ShapeDtypeStruct(found, F32),
            jax.ShapeDtypeStruct((MIXED, BRICK, TILES * ROWS), BF),
        ),
        scratch_shapes=[
            pltpu.VMEM(found, F32),
            pltpu.VMEM((2, ALONG, 3 * 256), BF),
            pltpu.VMEM((MIXED * BRICK, 128), F32),
            pltpu.VMEM((MIXED * BRICK, 128), F32),
            pltpu.VMEM(banded.shape, BF),
            pltpu.SemaphoreType.DMA((2,)),
        ],
        name="finish",
        interpret=interpret,
    )(place, own, got, high, low, spread, banded, biases, projected)


def close(value):
    return pltpu.with_memory_space_constraint(value, pltpu.VMEM)


def body(
    raw_tiles, ref_bands, shifts, matrix_ids, resample, unmix, conv_weight, conv_bias, out_weight
):
    high, low = tables()
    swap = functools.partial(
        lax.all_to_all, axis_name=("round", "tile"), split_axis=0, concat_axis=0, tiled=True
    )
    place = jnp.stack([lax.axis_index("round") >> 2, lax.axis_index("tile") & 1])
    place = close(jnp.broadcast_to(place[:, None, None], (2, 8, WIDTH)))
    band = close(ref_bands[0])
    ahead = [(i, (i + FAR) % ROUNDS) for i in range(ROUNDS)]
    other = close(lax.ppermute(band, "round", ahead))
    spread, banded, biases, projected = prepare(
        unmix, conv_weight, conv_bias.reshape(1, -1), out_weight
    )
    spread, biases, projected = map(close, (spread, biases, projected))
    high, low = close(jnp.asarray(high)), close(jnp.asarray(low))
    sent, own = warp(shifts, matrix_ids, raw_tiles[0], resample)
    got = close(swap(sent, axis_index_groups=RINGS))
    slabs = close(swap(regroup(got, band, other), axis_index_groups=NEAR))
    spectra = close(own_spectra(close(own), high, low))
    correlation, features = finish(
        place, spectra, slabs, high, low, spread, banded, biases, projected
    )
    return (correlation[None], features[:, None])


def solution(mesh):
    placed = (
        P("round", None, None, "tile", None),
        P("round", "tile", None),
        P("round", "tile"),
        P("round", None),
        P(),
        P(),
        P(),
        P(),
        P(),
    )
    return jax.shard_map(
        body,
        mesh=mesh,
        in_specs=placed,
        out_specs=(P("round", None, None, "tile", None), P(None, "round", "tile", None)),
        check_vma=False,
    )
```

```python
import functools
import math

import jax
import jax.numpy as jnp
import numpy as np
from jax import lax
from jax.experimental import pallas as pl
from jax.experimental.pallas import tpu as pltpu
from jax.sharding import PartitionSpec as P

BF = jnp.bfloat16
F32 = jnp.float32
ROUNDS, TILES = 8, 64
CH, DEPTH, ROWS, WIDTH = 4, 8, 4, 512
MIXED, HIDDEN = 32, 64
HALVES, FAR = 2, 4
PAIRS = TILES // 2
PLANE = CH * ROWS
BRICK = WIDTH // TILES
SPAN = BRICK + 2
LINES = 3 * HALVES * PLANE
ALONG = SPAN * PAIRS
PADDED = 384
SMALL = 9 * 256


def device(half, far, pair, core):
    return (half * FAR + far) * TILES + 2 * pair + core


RINGS = [
    [device(half, far, pair, core) for half in range(HALVES) for pair in range(PAIRS)]
    for far in range(FAR)
    for core in range(2)
]
NEAR = [
    [device(half, far, pair, core) for far in range(FAR) for core in range(2)]
    for half in range(HALVES)
    for pair in range(PAIRS)
]


def iota(shape, dim):
    return lax.broadcasted_iota(jnp.int32, shape, dim)


def dot(a, b, dims):
    return lax.dot_general(a, b, (dims, ((), ())), preferred_element_type=F32)


def warp_kernel(shift, ids, tiles, table, out, own, raw, mats, chosen, sent, sems):
    inward = [
        pltpu.make_async_copy(tiles, raw, sems.at[0, 0]),
        pltpu.make_async_copy(ids, chosen, sems.at[1, 0]),
    ]
    inward += [
        pltpu.make_async_copy(
            table.at[k, pl.ds(at, 128)], mats.at[k, pl.ds(at, 128)], sems.at[2 + k, at // 128]
        )
        for k in range(CH)
        for at in range(0, WIDTH, 128)
    ]
    for copy in inward:
        copy.start()
    by = shift[0, 0]
    inward[0].wait()
    turned = []
    for c in range(CH):
        rows = jnp.concatenate([raw[c, z].astype(F32) for z in range(DEPTH)], axis=0)
        turned.append(pltpu.roll(rows, by, 1).astype(BF))
    for copy in inward[1:]:
        copy.wait()
    warped = []
    for c in range(CH):
        result = dot(turned[c], mats[chosen[0, c]], ((1,), (0,)))
        own[c] = result.astype(BF)
        warped.append(result.reshape(DEPTH // 2, 2 * ROWS, WIDTH))
    low = iota((DEPTH // 2, 2 * ROWS, WIDTH), 1) < ROWS
    even, odd = [], []
    for c in range(0, CH, 2):
        a, b = warped[c], warped[c + 1]
        even.append(jnp.where(low, a, pltpu.roll(b, ROWS, 1)))
        odd.append(jnp.where(low, pltpu.roll(a, ROWS, 1), b))
    planes = []
    for z in range(DEPTH):
        planes += [p[z // 2] for p in (odd if z % 2 else even)]
    upright = jnp.concatenate(planes, axis=0).T.reshape(PAIRS, 2, BRICK, DEPTH * PLANE)
    left, right = upright[:, 0], upright[:, 1]
    edge = jnp.zeros((1, BRICK, DEPTH * PLANE), F32)
    before = jnp.concatenate([edge, right[:-1]], axis=0)
    after = jnp.concatenate([left[1:], edge], axis=0)
    row, lane = iota(left.shape, 1), iota(left.shape, 2)

    def put(base, value, start, to, width, only=None, turn=0):
        value = pltpu.roll(value, turn, 1) if turn else value
        value = pltpu.roll(value, (to - start) % 128, 2) if to != start else value
        here = (lane >= to) & (lane < to + width)
        return jnp.where(here if only is None else here & (row == only), value, base)

    outward = []
    for half in range(HALVES):
        start = 64 * half
        main = put(left, right, start, 64, 64) if half == 0 else put(right, left, start, 0, 64)
        more = jnp.zeros(left.shape, F32)
        more = put(more, before, start, 64, 64, 0, 1)
        more = put(more, after, start, 64, 64, 1, 1)
        outer = 64 if half == 0 else 48
        slot = 32 if half == 0 else 0
        more = put(more, left, outer, slot, PLANE)
        more = put(more, right, outer, slot + PLANE, PLANE)
        more = put(more, before, outer, 64 + slot // 2, PLANE, 2, 3)
        more = put(more, after, outer, 96 + slot // 2, PLANE, 2, 2)
        part = slice(half * PAIRS, (half + 1) * PAIRS)
        sent[part] = jnp.concatenate([main, more], axis=1).astype(BF)
        copy = pltpu.make_async_copy(sent.at[part], out.at[part], sems.at[6 + half, 0])
        copy.start()
        outward.append(copy)
    for copy in outward:
        copy.wait()


def warp(shift, ids, raw, table, interpret=False):
    away = pl.BlockSpec(memory_space=pl.ANY)
    shape = (TILES, 2 * BRICK, DEPTH * PLANE)
    return pl.pallas_call(
        warp_kernel,
        out_shape=(
            jax.ShapeDtypeStruct(shape, BF),
            pltpu.VMEM((CH, DEPTH * ROWS, WIDTH), BF),
        ),
        in_specs=[pl.BlockSpec(memory_space=pltpu.SMEM), away, away, away],
        out_specs=(away, pl.BlockSpec(memory_space=pltpu.VMEM)),
        scratch_shapes=[
            pltpu.VMEM(raw.shape, BF),
            pltpu.VMEM(table.shape, BF),
            pltpu.SMEM(ids.shape, jnp.int32),
            pltpu.VMEM(shape, BF),
            pltpu.SemaphoreType.DMA((8, 4)),
        ],
        name="warp",
        interpret=interpret,
    )(shift, ids, raw, table)


def prepare_kernel(unmix, conv, project, own, high, low, banded, spectra):
    rows = own[...].reshape(CH * DEPTH * ROWS, WIDTH)
    spectra[...] = dot(rows, high[...], ((1,), (0,))) + dot(rows, low[...], ((1,), (0,)))
    n = MIXED * ROWS
    k = iota((n, MIXED), 0)
    source = (k // PLANE % HALVES * FAR + k // (HALVES * PLANE)) * CH + k // ROWS % CH
    pick_in = (source == iota((n, MIXED), 1)).astype(BF)
    pick_out = (iota((MIXED, n), 1) % MIXED == iota((MIXED, n), 0)).astype(BF)
    tall = dot(pick_in, unmix[...], ((1,), (1,))).astype(BF)
    wide = dot(tall, pick_out, ((1,), (0,)))
    own = iota((n, n), 0) % ROWS == iota((n, n), 1) // MIXED
    banded[n:, SMALL : SMALL + n] = jnp.where(own, wide, 0.0).astype(BF)
    banded[n:, SMALL + n :] = jnp.zeros((n, n), BF)
    gap = jnp.zeros((HIDDEN, MIXED), BF)
    for ab in range(9):
        at = (ab % 3 * 3 + ab // 3) * 256
        d = [conv[3 * ab + i] for i in range(3)]
        rows = [
            [d[1], d[2], gap, gap, gap, gap, gap, d[0]],
            [d[0], d[1], d[2], gap, gap, gap, gap, gap],
            [gap, d[0], d[1], d[2], gap, gap, gap, gap],
            [gap, gap, d[0], d[1], d[2], gap, gap, gap],
        ]
        for y in range(ROWS):
            banded[y * HIDDEN : (y + 1) * HIDDEN, at : at + 256] = jnp.concatenate(
                rows[y], axis=1
            )
    hole = jnp.zeros((MIXED, HIDDEN), BF)
    for y in range(ROWS):
        row = [project[...] if i == y else hole for i in range(ROWS)]
        banded[y * MIXED : (y + 1) * MIXED, SMALL:] = jnp.concatenate(row, axis=1)


def prepare(unmix, conv, project, own, high, low, interpret=False):
    return pl.pallas_call(
        prepare_kernel,
        out_shape=(
            pltpu.VMEM((HIDDEN * ROWS, SMALL + 256), BF),
            pltpu.HBM((CH * DEPTH * ROWS, WIDTH), F32),
        ),
        compiler_params=pltpu.CompilerParams(vmem_limit_bytes=16 << 20),
        name="prepare",
        interpret=interpret,
    )(unmix, conv, project, own, high, low)


def regroup_kernel(got, band, other, out, tall, sent, sems):
    tall[...] = got[...].astype(F32).reshape(TILES * 2 * BRICK, DEPTH * PLANE)
    turned = []
    for q in range(BRICK):
        both = [tall[pl.ds(q + at, TILES, stride=2 * BRICK), :] for at in (0, BRICK)]
        turned.append(jnp.concatenate(both, axis=0).T)

    def piece(slot, column):
        x = column - 1
        if 0 <= x < 2 * BRICK:
            block, q = x // BRICK, x % BRICK
            if 1 <= slot <= 4:
                start, at = block * 64 + (slot - 1) * PLANE, 0
            else:
                start, at = (32 if slot else 0) + block * PLANE, 64
        else:
            side = 0 if x < 0 else 1
            if 1 <= slot <= 4:
                q, start, at = side, 64 + (slot - 1) * PLANE, 64
            else:
                q, start, at = 2, 64 + 32 * side + (PLANE if slot else 0), 64
        return turned[q][start : start + PLANE], at

    refs = jnp.concatenate([band[...].astype(F32), other[...].astype(F32)], axis=0)
    marks = []
    for p in range(0, 8, 2):
        pair = refs[:, p * 64 : (p + 2) * 64]
        marks.append(jnp.concatenate([pltpu.roll(pair, 64, 1), pair], axis=0))
    lane = iota((PLANE, 128), 1)
    outward = []
    for core in range(2):
        for slot in range(6):
            pieces = [piece(slot, core * BRICK + k) for k in range(SPAN)]
            for half in range(HALVES):
                blocks = []
                for m in range(3):
                    block = jnp.zeros((PLANE, 128), F32)
                    for k in range(4 * m, min(4 * m + 4, SPAN)):
                        rows, at = pieces[k]
                        to = k % 4 * PAIRS
                        turn = (to - at - half * PAIRS) % 128
                        rows = pltpu.roll(rows, turn, 1) if turn else rows
                        block = jnp.where((lane >= to) & (lane < to + PAIRS), rows, block)
                    blocks.append(block)
                main = [block.astype(BF) for block in blocks[:2]]
                for far in range(FAR):
                    step = slot - far
                    if not 0 <= step < 3:
                        continue
                    w = step * HALVES + half
                    last = jnp.where(lane >= 64, marks[w], blocks[2]) if w < 4 else blocks[2]
                    rows = slice(w * PLANE, (w + 1) * PLANE)
                    sent[2 * far + core, rows, :128] = main[0]
                    sent[2 * far + core, rows, 128:256] = main[1]
                    sent[2 * far + core, rows, 256:] = last.astype(BF)
            if slot >= 2:
                peer = 2 * (slot - 2) + core
                copy = pltpu.make_async_copy(sent.at[peer], out.at[peer], sems.at[peer])
                copy.start()
                outward.append(copy)
    for copy in outward:
        copy.wait()


def regroup(got, band, other, interpret=False):
    shape = (2 * FAR, LINES, PADDED)
    return pl.pallas_call(
        regroup_kernel,
        out_shape=jax.ShapeDtypeStruct(shape, BF),
        in_specs=[pl.BlockSpec(memory_space=pltpu.VMEM)] * 3,
        out_specs=pl.BlockSpec(memory_space=pl.ANY),
        scratch_shapes=[
            pltpu.VMEM((TILES * 2 * BRICK, DEPTH * PLANE), F32),
            pltpu.VMEM(shape, BF),
            pltpu.SemaphoreType.DMA((2 * FAR,)),
        ],
        name="regroup",
        compiler_params=pltpu.CompilerParams(vmem_limit_bytes=16 << 20),
        interpret=interpret,
    )(got, band, other)


def tables():
    x = np.arange(WIDTH, dtype=np.int64)
    half = WIDTH // 2
    frequency = np.where(x < half, x, np.where(x == half, half, x - half))
    angles = (x[:, None] * frequency[None, :] % WIDTH) * (2.0 * math.pi / WIDTH)
    table = np.where((x <= half)[None, :], np.cos(angles), np.sin(angles)).astype(np.float32)
    high = table.astype(jnp.bfloat16)
    low = (table - high.astype(np.float32)).astype(jnp.bfloat16)
    return high, low


def correlate(place, own, got, high, low, out):
    half = WIDTH // 2
    count = CH * DEPTH * ROWS
    left = iota((2 * ROWS, 128), 1) < 64
    near, away = [], []
    for far in range(FAR):
        pieces = jnp.where(
            place[1, :1, :128] == 0,
            got[2 * far, :64, 256:].astype(F32),
            got[2 * far + 1, :64, 256:].astype(F32),
        )
        lanes = []
        for p in range(0, 8, 2):
            a = pieces[p * 2 * ROWS : (p + 1) * 2 * ROWS]
            b = pieces[(p + 1) * 2 * ROWS : (p + 2) * 2 * ROWS]
            lanes.append(jnp.where(left, pltpu.roll(a, 64, 1), b))
        rows = jnp.concatenate(lanes, axis=1)
        near.append(rows[:ROWS])
        away.append(rows[ROWS:])
    near, away = jnp.concatenate(near, axis=0), jnp.concatenate(away, axis=0)
    first_half = place[0, :1, :] == 0
    band = jnp.concatenate(
        [jnp.where(first_half, near, away), jnp.where(first_half, away, near)], axis=0
    ).astype(BF)
    along = ((1,), (0,))
    band = dot(band, high[...], along) + dot(band, low[...], along)
    own_cos = own[:, :half].reshape(CH, DEPTH * ROWS, half)
    own_sin = own[:, half:].reshape(CH, DEPTH * ROWS, half)
    band_cos = band[:, :half]
    band_sin = band[:, half:]
    first = iota(own_cos.shape, 2) == 0
    sines = own_sin * band_sin
    cosines = own_cos * band_cos
    real = jnp.where(first, cosines, 2.0 * (cosines + sines))
    imag = jnp.where(first, sines, 2.0 * (own_sin * band_cos - own_cos * band_sin))
    joined = jnp.concatenate([real.reshape(count, half), imag.reshape(count, half)], axis=1)
    upper = joined.astype(BF)
    lower = (joined - upper.astype(F32)).astype(BF)
    across = ((1,), (1,))
    both = dot(jnp.concatenate([upper, lower], axis=0), high[...], across)
    inverse = both[:count] + both[count:] + dot(upper, low[...], across)
    inverse = inverse * (1.0 / (WIDTH * math.sqrt(WIDTH)))
    for c in range(CH):
        for z in range(DEPTH):
            start = (c * DEPTH + z) * ROWS
            out[c, z] = inverse[start : start + ROWS]


def finish_kernel(
    place, spectra, got, high, low, banded, bias, away, out,
    found, wide, first, second, own, shared, sems,
):
    fetch = [
        pltpu.make_async_copy(spectra, own, sems.at[2]),
        pltpu.make_async_copy(bias, shared, sems.at[1]),
    ]
    for copy in fetch:
        copy.start()
    n = MIXED * ROWS
    pair = iota((SPAN, PAIRS, n), 1).reshape(ALONG, n)
    right = iota((ALONG, n), 1) >= 64
    count = BRICK * PAIRS
    centre = None
    for a in range(3):
        at = a * 256
        planes = []
        for core in range(2):
            mixed = jnp.concatenate(
                [
                    got[2 * far + core, a * HALVES * PLANE : (a + 1) * HALVES * PLANE, :]
                    for far in range(FAR)
                ],
                axis=0,
            )
            plane = dot(mixed, banded[n:, SMALL : SMALL + n], ((0,), (0,)))[:ALONG].astype(BF)
            wide[core, :, at : at + 128] = plane
            planes.append(plane.astype(F32))
        even, odd = planes
        if a == 1:
            centre = jnp.concatenate([p[PAIRS : PAIRS + count] for p in planes], axis=0)
        upper = jnp.where(pair == 0, 0.0, pltpu.roll(odd, 1, 0))
        lower = jnp.where(pair == PAIRS - 1, 0.0, pltpu.roll(even, ALONG - 1, 0))
        wide[0, :, at + 128 : at + 256] = jnp.where(right, upper, odd).astype(BF)
        wide[1, :, at + 128 : at + 256] = jnp.where(right, even, lower).astype(BF)
    for copy in fetch:
        copy.wait()
    correlate(place, own, got, high, low, found)
    leave = pltpu.make_async_copy(found, away, sems.at[0])
    leave.start()
    total = jnp.concatenate([shared[...]] * ROWS, axis=1)
    for b in range(3):
        rows = jnp.concatenate(
            [wide[core, b * PAIRS : b * PAIRS + count, :] for core in range(2)], axis=0
        )
        total = total + dot(rows, banded[:, b * 768 : (b + 1) * 768], ((1,), (1,)))
    hidden = jax.nn.gelu(total).astype(BF)
    mixed = dot(hidden, banded[:n, SMALL:], ((1,), (1,)))
    done = centre + mixed
    left = iota((MIXED, 128), 1) < 64
    k = iota((256, 256), 0)
    order = iota((256, 256), 1) == 8 * (k % PAIRS) + 4 * (k // PAIRS % 2) + k // 64
    order = order.astype(BF)
    lines = []
    for x in range(0, BRICK, 2):
        pair = jnp.concatenate(
            [
                done[core * count + at * PAIRS : core * count + (at + 1) * PAIRS]
                for at in (x, x + 1)
                for core in range(2)
            ],
            axis=0,
        ).T
        y = [pair[i * MIXED : (i + 1) * MIXED, :] for i in range(ROWS)]
        lines.append(
            jnp.concatenate(
                [
                    jnp.where(left, y[0], pltpu.roll(y[1], 64, 1)),
                    jnp.where(left, y[2], pltpu.roll(y[3], 64, 1)),
                ],
                axis=1,
            )
        )
        lines.append(
            jnp.concatenate(
                [
                    jnp.where(left, pltpu.roll(y[0], 64, 1), y[1]),
                    jnp.where(left, pltpu.roll(y[2], 64, 1), y[3]),
                ],
                axis=1,
            )
        )
    ordered = dot(jnp.concatenate(lines, axis=0).astype(BF), order, ((1,), (0,)))
    for x in range(BRICK):
        rows = ordered[x * MIXED : (x + 1) * MIXED]
        first[pl.ds(x, MIXED, stride=BRICK), :] = rows[:, :128]
        second[pl.ds(x, MIXED, stride=BRICK), :] = rows[:, 128:]
    out[:, :, :128] = first[...].reshape(MIXED, BRICK, 128).astype(BF)
    out[:, :, 128:] = second[...].reshape(MIXED, BRICK, 128).astype(BF)
    leave.wait()


def finish(place, own, got, high, low, banded, bias, interpret=False):
    inside = pl.BlockSpec(memory_space=pltpu.VMEM)
    outside = pl.BlockSpec(memory_space=pl.ANY)
    found = (CH, DEPTH, ROWS, WIDTH)
    return pl.pallas_call(
        finish_kernel,
        in_specs=[inside, pl.BlockSpec(memory_space=pltpu.HBM)] + [inside] * 4 + [outside],
        out_specs=(outside, inside),
        out_shape=(
            jax.ShapeDtypeStruct(found, F32),
            jax.ShapeDtypeStruct((MIXED, BRICK, TILES * ROWS), BF),
        ),
        scratch_shapes=[
            pltpu.VMEM(found, F32),
            pltpu.VMEM((2, ALONG, 3 * 256), BF),
            pltpu.VMEM((MIXED * BRICK, 128), F32),
            pltpu.VMEM((MIXED * BRICK, 128), F32),
            pltpu.VMEM(own.shape, F32),
            pltpu.VMEM(bias.shape, F32),
            pltpu.SemaphoreType.DMA((3,)),
        ],
        name="finish",
        compiler_params=pltpu.CompilerParams(vmem_limit_bytes=16 << 20),
        interpret=interpret,
    )(place, own, got, high, low, banded, bias)


def close(value):
    return pltpu.with_memory_space_constraint(value, pltpu.VMEM)


def body(
    raw_tiles, ref_bands, shifts, matrix_ids, resample, unmix, conv_weight, conv_bias, out_weight
):
    high, low = tables()
    swap = functools.partial(
        lax.all_to_all, axis_name=("round", "tile"), split_axis=0, concat_axis=0, tiled=True
    )
    place = jnp.stack([lax.axis_index("round") >> 2, lax.axis_index("tile") & 1])
    place = close(jnp.broadcast_to(place[:, None, None], (2, 8, WIDTH)))
    band = close(ref_bands[0])
    ahead = [(i, (i + FAR) % ROUNDS) for i in range(ROUNDS)]
    other = close(lax.ppermute(band, "round", ahead))
    high, low = close(jnp.asarray(high)), close(jnp.asarray(low))
    sent, own = warp(shifts, matrix_ids, raw_tiles[0], resample)
    got = close(swap(sent, axis_index_groups=RINGS))
    slabs = close(swap(regroup(got, band, other), axis_index_groups=NEAR))
    prepared = prepare(unmix, conv_weight, out_weight, close(own), high, low)
    banded = close(prepared[0])
    spectra = pltpu.with_memory_space_constraint(prepared[1], pltpu.HBM)
    bias = conv_bias.reshape(1, -1)
    correlation, features = finish(place, spectra, slabs, high, low, banded, bias)
    return (correlation[None], features[:, None])


def solution(mesh):
    placed = (
        P("round", None, None, "tile", None),
        P("round", "tile", None),
        P("round", "tile"),
        P("round", None),
        P(),
        P(),
        P(),
        P(),
        P(),
    )
    return jax.shard_map(
        body,
        mesh=mesh,
        in_specs=placed,
        out_specs=(P("round", None, None, "tile", None), P(None, "round", "tile", None)),
        check_vma=False,
    )
```

```python
import functools
import math

import jax
import jax.numpy as jnp
import numpy as np
from jax import lax
from jax.experimental import pallas as pl
from jax.experimental.pallas import tpu as pltpu
from jax.sharding import PartitionSpec as P

BF = jnp.bfloat16
F32 = jnp.float32
ROUNDS, TILES = 8, 64
CH, DEPTH, ROWS, WIDTH = 4, 8, 4, 512
MIXED, HIDDEN = 32, 64
HALVES, FAR = 2, 4
PAIRS = TILES // 2
PLANE = CH * ROWS
BRICK = WIDTH // TILES
SPAN = BRICK + 2
LINES = 3 * HALVES * PLANE
ALONG = SPAN * PAIRS
PADDED = 384
SMALL = 9 * 256


def device(half, far, pair, core):
    return (half * FAR + far) * TILES + 2 * pair + core


RINGS = [
    [device(half, far, pair, core) for half in range(HALVES) for pair in range(PAIRS)]
    for far in range(FAR)
    for core in range(2)
]
NEAR = [
    [device(half, far, pair, core) for far in range(FAR) for core in range(2)]
    for half in range(HALVES)
    for pair in range(PAIRS)
]


def iota(shape, dim):
    return lax.broadcasted_iota(jnp.int32, shape, dim)


def dot(a, b, dims):
    return lax.dot_general(a, b, (dims, ((), ())), preferred_element_type=F32)


def warp_kernel(shift, ids, tiles, table, out, own, raw, mats, chosen, sent, sems):
    inward = [
        pltpu.make_async_copy(tiles, raw, sems.at[0]),
        pltpu.make_async_copy(ids, chosen, sems.at[1]),
    ]
    inward += [
        pltpu.make_async_copy(table.at[k], mats.at[k], sems.at[2 + k]) for k in range(CH)
    ]
    for copy in inward:
        copy.start()
    by = shift[0, 0]
    inward[0].wait()
    turned = []
    for c in range(CH):
        rows = jnp.concatenate([raw[c, z].astype(F32) for z in range(DEPTH)], axis=0)
        turned.append(pltpu.roll(rows, by, 1).astype(BF))
    for copy in inward[1:]:
        copy.wait()
    warped = []
    for c in range(CH):
        result = dot(turned[c], mats[chosen[0, c]], ((1,), (0,)))
        own[c] = result.astype(BF)
        warped.append(result.reshape(DEPTH // 2, 2 * ROWS, WIDTH))
    low = iota((DEPTH // 2, 2 * ROWS, WIDTH), 1) < ROWS
    even, odd = [], []
    for c in range(0, CH, 2):
        a, b = warped[c], warped[c + 1]
        even.append(jnp.where(low, a, pltpu.roll(b, ROWS, 1)))
        odd.append(jnp.where(low, pltpu.roll(a, ROWS, 1), b))
    planes = []
    for z in range(DEPTH):
        planes += [p[z // 2] for p in (odd if z % 2 else even)]
    upright = jnp.concatenate(planes, axis=0).T.reshape(PAIRS, 2, BRICK, DEPTH * PLANE)
    left, right = upright[:, 0], upright[:, 1]
    edge = jnp.zeros((1, BRICK, DEPTH * PLANE), F32)
    before = jnp.concatenate([edge, right[:-1]], axis=0)
    after = jnp.concatenate([left[1:], edge], axis=0)
    row, lane = iota(left.shape, 1), iota(left.shape, 2)

    def put(base, value, start, to, width, only=None, turn=0):
        value = pltpu.roll(value, turn, 1) if turn else value
        value = pltpu.roll(value, (to - start) % 128, 2) if to != start else value
        here = (lane >= to) & (lane < to + width)
        return jnp.where(here if only is None else here & (row == only), value, base)

    outward = []
    for half in range(HALVES):
        start = 64 * half
        main = put(left, right, start, 64, 64) if half == 0 else put(right, left, start, 0, 64)
        more = jnp.zeros(left.shape, F32)
        more = put(more, before, start, 64, 64, 0, 1)
        more = put(more, after, start, 64, 64, 1, 1)
        outer = 64 if half == 0 else 48
        slot = 32 if half == 0 else 0
        more = put(more, left, outer, slot, PLANE)
        more = put(more, right, outer, slot + PLANE, PLANE)
        more = put(more, before, outer, 64 + slot // 2, PLANE, 2, 3)
        more = put(more, after, outer, 96 + slot // 2, PLANE, 2, 2)
        part = slice(half * PAIRS, (half + 1) * PAIRS)
        sent[part] = jnp.concatenate([main, more], axis=1).astype(BF)
        copy = pltpu.make_async_copy(sent.at[part], out.at[part], sems.at[6 + half])
        copy.start()
        outward.append(copy)
    for copy in outward:
        copy.wait()


def warp(shift, ids, raw, table, interpret=False):
    away = pl.BlockSpec(memory_space=pl.ANY)
    shape = (TILES, 2 * BRICK, DEPTH * PLANE)
    return pl.pallas_call(
        warp_kernel,
        out_shape=(
            jax.ShapeDtypeStruct(shape, BF),
            pltpu.VMEM((CH, DEPTH * ROWS, WIDTH), BF),
        ),
        in_specs=[pl.BlockSpec(memory_space=pltpu.SMEM), away, away, away],
        out_specs=(away, pl.BlockSpec(memory_space=pltpu.VMEM)),
        scratch_shapes=[
            pltpu.VMEM(raw.shape, BF),
            pltpu.VMEM(table.shape, BF),
            pltpu.SMEM(ids.shape, jnp.int32),
            pltpu.VMEM(shape, BF),
            pltpu.SemaphoreType.DMA((8,)),
        ],
        name="warp",
        interpret=interpret,
    )(shift, ids, raw, table)


def prepare_kernel(unmix, conv, project, banded):
    n = MIXED * ROWS
    k = iota((n, MIXED), 0)
    source = (k // PLANE % HALVES * FAR + k // (HALVES * PLANE)) * CH + k // ROWS % CH
    pick_in = (source == iota((n, MIXED), 1)).astype(BF)
    pick_out = (iota((MIXED, n), 1) % MIXED == iota((MIXED, n), 0)).astype(BF)
    tall = dot(pick_in, unmix[...], ((1,), (1,))).astype(BF)
    wide = dot(tall, pick_out, ((1,), (0,)))
    own = iota((n, n), 0) % ROWS == iota((n, n), 1) // MIXED
    banded[n:, SMALL : SMALL + n] = jnp.where(own, wide, 0.0).astype(BF)
    banded[n:, SMALL + n :] = jnp.zeros((n, n), BF)
    gap = jnp.zeros((HIDDEN, MIXED), BF)
    for ab in range(9):
        at = (ab % 3 * 3 + ab // 3) * 256
        d = [conv[3 * ab + i] for i in range(3)]
        rows = [
            [d[1], d[2], gap, gap, gap, gap, gap, d[0]],
            [d[0], d[1], d[2], gap, gap, gap, gap, gap],
            [gap, d[0], d[1], d[2], gap, gap, gap, gap],
            [gap, gap, d[0], d[1], d[2], gap, gap, gap],
        ]
        for y in range(ROWS):
            banded[y * HIDDEN : (y + 1) * HIDDEN, at : at + 256] = jnp.concatenate(
                rows[y], axis=1
            )
    hole = jnp.zeros((MIXED, HIDDEN), BF)
    halved = (0.5 * project[...].astype(F32)).astype(BF)
    for y in range(ROWS):
        row = [halved if i == y else hole for i in range(ROWS)]
        banded[y * MIXED : (y + 1) * MIXED, SMALL:] = jnp.concatenate(row, axis=1)


def prepare(unmix, conv, project, interpret=False):
    return pl.pallas_call(
        prepare_kernel,
        out_shape=pltpu.VMEM((HIDDEN * ROWS, SMALL + 256), BF),
        compiler_params=pltpu.CompilerParams(vmem_limit_bytes=16 << 20),
        name="prepare",
        interpret=interpret,
    )(unmix, conv, project)


def regroup_kernel(got, bands, out, passed, tall, sent, sems):
    passed[...] = bands[...]
    tall[...] = got[...].astype(F32).reshape(TILES * 2 * BRICK, DEPTH * PLANE)
    turned = []
    for q in range(BRICK):
        both = [tall[pl.ds(q + at, TILES, stride=2 * BRICK), :] for at in (0, BRICK)]
        turned.append(jnp.concatenate(both, axis=0).T)

    def piece(slot, column):
        x = column - 1
        if 0 <= x < 2 * BRICK:
            block, q = x // BRICK, x % BRICK
            if 1 <= slot <= 4:
                start, at = block * 64 + (slot - 1) * PLANE, 0
            else:
                start, at = (32 if slot else 0) + block * PLANE, 64
        else:
            side = 0 if x < 0 else 1
            if 1 <= slot <= 4:
                q, start, at = side, 64 + (slot - 1) * PLANE, 64
            else:
                q, start, at = 2, 64 + 32 * side + (PLANE if slot else 0), 64
        return turned[q][start : start + PLANE], at

    lane = iota((PLANE, 128), 1)
    outward = []
    for core in range(2):
        for slot in range(6):
            pieces = [piece(slot, core * BRICK + k) for k in range(SPAN)]
            for half in range(HALVES):
                blocks = []
                for m in range(3):
                    block = jnp.zeros((PLANE, 128), F32)
                    for k in range(4 * m, min(4 * m + 4, SPAN)):
                        rows, at = pieces[k]
                        to = k % 4 * PAIRS
                        turn = (to - at - half * PAIRS) % 128
                        rows = pltpu.roll(rows, turn, 1) if turn else rows
                        block = jnp.where((lane >= to) & (lane < to + PAIRS), rows, block)
                    blocks.append(block)
                main = [block.astype(BF) for block in blocks]
                for far in range(FAR):
                    step = slot - far
                    if not 0 <= step < 3:
                        continue
                    w = step * HALVES + half
                    rows = slice(w * PLANE, (w + 1) * PLANE)
                    sent[2 * far + core, rows, :128] = main[0]
                    sent[2 * far + core, rows, 128:256] = main[1]
                    sent[2 * far + core, rows, 256:] = main[2]
            if slot >= 2:
                peer = 2 * (slot - 2) + core
                copy = pltpu.make_async_copy(sent.at[peer], out.at[peer], sems.at[peer])
                copy.start()
                outward.append(copy)
    for copy in outward:
        copy.wait()


def regroup(got, bands, interpret=False):
    shape = (2 * FAR, LINES, PADDED)
    return pl.pallas_call(
        regroup_kernel,
        out_shape=(jax.ShapeDtypeStruct(shape, BF), jax.ShapeDtypeStruct(bands.shape, BF)),
        in_specs=[pl.BlockSpec(memory_space=pltpu.VMEM)] * 2,
        out_specs=(pl.BlockSpec(memory_space=pl.ANY), pl.BlockSpec(memory_space=pltpu.VMEM)),
        scratch_shapes=[
            pltpu.VMEM((TILES * 2 * BRICK, DEPTH * PLANE), F32),
            pltpu.VMEM(shape, BF),
            pltpu.SemaphoreType.DMA((2 * FAR,)),
        ],
        name="regroup",
        compiler_params=pltpu.CompilerParams(vmem_limit_bytes=16 << 20),
        interpret=interpret,
    )(got, bands)


def tables():
    x = np.arange(WIDTH, dtype=np.int64)
    half = WIDTH // 2
    frequency = np.where(x < half, x, np.where(x == half, half, x - half))
    angles = (x[:, None] * frequency[None, :] % WIDTH) * (2.0 * math.pi / WIDTH)
    table = np.where((x <= half)[None, :], np.cos(angles), np.sin(angles)).astype(np.float32)
    high = table.astype(jnp.bfloat16)
    low = (table - high.astype(np.float32)).astype(jnp.bfloat16)
    return high, low


def correlate_kernel(slots, own, bands, high, low, out):
    half = WIDTH // 2
    count = CH * DEPTH * ROWS
    band = jnp.concatenate([bands[slots[z]].astype(F32) for z in range(DEPTH)], axis=0).astype(BF)
    rows = jnp.concatenate([own[...].reshape(count, WIDTH), band], axis=0)
    along = ((1,), (0,))
    spectra = dot(rows, high[...], along) + dot(rows, low[...], along)
    own, band = spectra[:count], spectra[count:]
    own_cos = own[:, :half].reshape(CH, DEPTH * ROWS, half)
    own_sin = own[:, half:].reshape(CH, DEPTH * ROWS, half)
    band_cos = band[:, :half]
    band_sin = band[:, half:]
    first = iota(own_cos.shape, 2) == 0
    sines = own_sin * band_sin
    cosines = own_cos * band_cos
    real = jnp.where(first, cosines, 2.0 * (cosines + sines))
    imag = jnp.where(first, sines, 2.0 * (own_sin * band_cos - own_cos * band_sin))
    joined = jnp.concatenate([real.reshape(count, half), imag.reshape(count, half)], axis=1)
    upper = joined.astype(BF)
    lower = (joined - upper.astype(F32)).astype(BF)
    across = ((1,), (1,))
    both = dot(jnp.concatenate([upper, lower], axis=0), high[...], across)
    inverse = both[:count] + both[count:] + dot(upper, low[...], across)
    inverse = inverse * (1.0 / (WIDTH * math.sqrt(WIDTH)))
    for c in range(CH):
        for z in range(DEPTH):
            start = (c * DEPTH + z) * ROWS
            out[c, z] = inverse[start : start + ROWS]


def correlate(slots, own, bands, high, low, interpret=False):
    inside = pl.BlockSpec(memory_space=pltpu.VMEM)
    return pl.pallas_call(
        correlate_kernel,
        out_shape=jax.ShapeDtypeStruct((CH, DEPTH, ROWS, WIDTH), F32),
        in_specs=[pl.BlockSpec(memory_space=pltpu.SMEM)] + [inside] * 4,
        compiler_params=pltpu.CompilerParams(vmem_limit_bytes=16 << 20),
        name="correlate",
        interpret=interpret,
    )(slots, own, bands, high, low)


def finish_kernel(got, banded, bias, out, wide, first, second, shared, sems):
    fetch = pltpu.make_async_copy(bias, shared, sems.at[0])
    fetch.start()
    n = MIXED * ROWS
    pair = iota((SPAN, PAIRS, n), 1).reshape(ALONG, n)
    right = iota((ALONG, n), 1) >= 64
    count = BRICK * PAIRS
    centre = None
    for a in range(3):
        at = a * 256
        planes = []
        for core in range(2):
            mixed = jnp.concatenate(
                [
                    got[2 * far + core, a * HALVES * PLANE : (a + 1) * HALVES * PLANE, :]
                    for far in range(FAR)
                ],
                axis=0,
            )
            plane = dot(mixed, banded[n:, SMALL : SMALL + n], ((0,), (0,)))[:ALONG].astype(BF)
            wide[core, :, at : at + 128] = plane
            planes.append(plane.astype(F32))
        even, odd = planes
        if a == 1:
            centre = jnp.concatenate([p[PAIRS : PAIRS + count] for p in planes], axis=0)
        upper = jnp.where(pair == 0, 0.0, pltpu.roll(odd, 1, 0))
        lower = jnp.where(pair == PAIRS - 1, 0.0, pltpu.roll(even, ALONG - 1, 0))
        wide[0, :, at + 128 : at + 256] = jnp.where(right, upper, odd).astype(BF)
        wide[1, :, at + 128 : at + 256] = jnp.where(right, even, lower).astype(BF)
    fetch.wait()
    total = jnp.concatenate([shared[...]] * ROWS, axis=1)
    for b in range(3):
        rows = jnp.concatenate(
            [wide[core, b * PAIRS : b * PAIRS + count, :] for core in range(2)], axis=0
        )
        total = total + dot(rows, banded[:, b * 768 : (b + 1) * 768], ((1,), (1,)))
    slope = math.sqrt(2.0 / math.pi)
    hidden = total + total * jnp.tanh(total * (slope + slope * 0.044715 * (total * total)))
    hidden = hidden.astype(BF)
    mixed = dot(hidden, banded[:n, SMALL:], ((1,), (1,)))
    done = centre + mixed
    left = iota((MIXED, 128), 1) < 64
    k = iota((256, 256), 0)
    order = iota((256, 256), 1) == 8 * (k % PAIRS) + 4 * (k // PAIRS % 2) + k // 64
    order = order.astype(BF)
    lines = []
    for x in range(0, BRICK, 2):
        pair = jnp.concatenate(
            [
                done[core * count + at * PAIRS : core * count + (at + 1) * PAIRS]
                for at in (x, x + 1)
                for core in range(2)
            ],
            axis=0,
        ).T
        y = [pair[i * MIXED : (i + 1) * MIXED, :] for i in range(ROWS)]
        lines.append(
            jnp.concatenate(
                [
                    jnp.where(left, y[0], pltpu.roll(y[1], 64, 1)),
                    jnp.where(left, y[2], pltpu.roll(y[3], 64, 1)),
                ],
                axis=1,
            )
        )
        lines.append(
            jnp.concatenate(
                [
                    jnp.where(left, pltpu.roll(y[0], 64, 1), y[1]),
                    jnp.where(left, pltpu.roll(y[2], 64, 1), y[3]),
                ],
                axis=1,
            )
        )
    ordered = dot(jnp.concatenate(lines, axis=0).astype(BF), order, ((1,), (0,)))
    for x in range(BRICK):
        rows = ordered[x * MIXED : (x + 1) * MIXED]
        first[pl.ds(x, MIXED, stride=BRICK), :] = rows[:, :128]
        second[pl.ds(x, MIXED, stride=BRICK), :] = rows[:, 128:]
    out[:, :, :128] = first[...].reshape(MIXED, BRICK, 128).astype(BF)
    out[:, :, 128:] = second[...].reshape(MIXED, BRICK, 128).astype(BF)


def finish(got, banded, bias, interpret=False):
    inside = pl.BlockSpec(memory_space=pltpu.VMEM)
    return pl.pallas_call(
        finish_kernel,
        in_specs=[inside, inside, pl.BlockSpec(memory_space=pltpu.HBM)],
        out_shape=jax.ShapeDtypeStruct((MIXED, BRICK, TILES * ROWS), BF),
        scratch_shapes=[
            pltpu.VMEM((2, ALONG, 3 * 256), BF),
            pltpu.VMEM((MIXED * BRICK, 128), F32),
            pltpu.VMEM((MIXED * BRICK, 128), F32),
            pltpu.VMEM(bias.shape, F32),
            pltpu.SemaphoreType.DMA((1,)),
        ],
        compiler_params=pltpu.CompilerParams(vmem_limit_bytes=16 << 20),
        name="finish",
        interpret=interpret,
    )(got, banded, bias)


def close(value):
    return pltpu.with_memory_space_constraint(value, pltpu.VMEM)


def body(
    raw_tiles, ref_bands, shifts, matrix_ids, resample, unmix, conv_weight, conv_bias, out_weight
):
    high, low = tables()
    swap = functools.partial(
        lax.all_to_all, axis_name=("round", "tile"), split_axis=0, concat_axis=0, tiled=True
    )
    high, low = close(jnp.asarray(high)), close(jnp.asarray(low))
    sent, own = warp(shifts, matrix_ids, raw_tiles[0], resample)
    got = close(swap(sent, axis_index_groups=RINGS))
    bands = ref_bands

    def doubled(bands, step):
        pairs = [(i, i ^ step) for i in range(ROUNDS)]
        return jnp.concatenate([bands, lax.ppermute(bands, "round", pairs)], axis=0)

    for step in (1, 2):
        bands = doubled(bands, step)
    slots = jnp.arange(ROUNDS, dtype=jnp.int32) ^ lax.axis_index("round")
    banded = close(prepare(unmix, conv_weight, out_weight))
    chunks, bands = regroup(got, bands)
    slabs = close(swap(chunks, axis_index_groups=NEAR))
    bands = doubled(bands, 4)
    correlation = correlate(slots, own, bands, high, low)
    bias = pltpu.with_memory_space_constraint(conv_bias.reshape(1, -1), pltpu.HBM)
    features = finish(slabs, banded, bias)
    return (correlation[None], features[:, None])


def solution(mesh):
    placed = (
        P("round", None, None, "tile", None),
        P("round", "tile", None),
        P("round", "tile"),
        P("round", None),
        P(),
        P(),
        P(),
        P(),
        P(),
    )
    return jax.shard_map(
        body,
        mesh=mesh,
        in_specs=placed,
        out_specs=(P("round", None, None, "tile", None), P(None, "round", "tile", None)),
        check_vma=False,
    )
```

```python
import functools
import math

import jax
import jax.numpy as jnp
import numpy as np
from jax import lax
from jax.experimental import pallas as pl
from jax.experimental.pallas import tpu as pltpu
from jax.sharding import PartitionSpec as P

BF = jnp.bfloat16
F32 = jnp.float32
ROUNDS, TILES = 8, 64
CH, DEPTH, ROWS, WIDTH = 4, 8, 4, 512
MIXED, HIDDEN = 32, 64
HALVES, FAR = 2, 4
PAIRS = TILES // 2
PLANE = CH * ROWS
BRICK = WIDTH // TILES
SPAN = BRICK + 2
LINES = 3 * HALVES * PLANE
ALONG = SPAN * PAIRS
PADDED = 384


def device(half, far, pair, core):
    return (half * FAR + far) * TILES + 2 * pair + core


RINGS = [
    [device(half, far, pair, core) for half in range(HALVES) for pair in range(PAIRS)]
    for far in range(FAR)
    for core in range(2)
]
NEAR = [
    [device(half, far, pair, core) for far in range(FAR) for core in range(2)]
    for half in range(HALVES)
    for pair in range(PAIRS)
]


def iota(shape, dim):
    return lax.broadcasted_iota(jnp.int32, shape, dim)


def dot(a, b, dims):
    return lax.dot_general(a, b, (dims, ((), ())), preferred_element_type=F32)


def warp_kernel(shift, ids, tiles, table, out, own, raw, mats, chosen, sent, sems):
    inward = [
        pltpu.make_async_copy(tiles, raw, sems.at[0]),
        pltpu.make_async_copy(ids, chosen, sems.at[1]),
    ]
    inward += [
        pltpu.make_async_copy(table.at[k], mats.at[k], sems.at[2 + k]) for k in range(len(mats))
    ]
    for copy in inward:
        copy.start()
    by = shift[0, 0]
    inward[0].wait()
    turned = []
    for c in range(CH):
        rows = jnp.concatenate([raw[c, z].astype(F32) for z in range(DEPTH)], axis=0)
        turned.append(pltpu.roll(rows, by, 1).astype(BF))
    for copy in inward[1:]:
        copy.wait()
    warped = []
    for c in range(CH):
        result = dot(turned[c], mats[chosen[0, c]], ((1,), (0,)))
        own[c] = result.astype(BF)
        warped.append(result.reshape(DEPTH // 2, 2 * ROWS, WIDTH))
    low = iota((DEPTH // 2, 2 * ROWS, WIDTH), 1) < ROWS
    even, odd = [], []
    for c in range(0, CH, 2):
        a, b = warped[c], warped[c + 1]
        even.append(jnp.where(low, a, pltpu.roll(b, ROWS, 1)))
        odd.append(jnp.where(low, pltpu.roll(a, ROWS, 1), b))
    planes = []
    for z in range(DEPTH):
        planes += [p[z // 2] for p in (odd if z % 2 else even)]
    upright = jnp.concatenate(planes, axis=0).T.reshape(PAIRS, 2, BRICK, DEPTH * PLANE)
    left, right = upright[:, 0], upright[:, 1]
    edge = jnp.zeros((1, BRICK, DEPTH * PLANE), F32)
    before = jnp.concatenate([edge, right[:-1]], axis=0)
    after = jnp.concatenate([left[1:], edge], axis=0)
    row, lane = iota(left.shape, 1), iota(left.shape, 2)

    def put(base, value, start, to, width, only=None, turn=0):
        value = pltpu.roll(value, turn, 1) if turn else value
        value = pltpu.roll(value, (to - start) % 128, 2) if to != start else value
        here = (lane >= to) & (lane < to + width)
        return jnp.where(here if only is None else here & (row == only), value, base)

    outward = []
    def gather(value, outer):
        turned = pltpu.roll(value, 128 - outer, 2)
        turned = pltpu.roll(turned, 0, 2, stride=PLANE, stride_axis=1)
        return jnp.sum(jnp.where(lane // PLANE == row, turned, 0.0), axis=1, keepdims=True)

    for half in range(HALVES):
        start = 64 * half
        main = put(left, right, start, 64, 64) if half == 0 else put(right, left, start, 0, 64)
        outer = 64 if half == 0 else 48
        more = jnp.where(row == 0, gather(left, outer), gather(right, outer))
        more = jnp.where(row < 2, more, 0.0)
        more = put(more, before, start, 0, 64, 2, 3)
        more = put(more, after, start, 64, 64, 2, 2)
        more = put(more, before, outer, 0, PLANE, 3, 4)
        more = put(more, after, outer, PLANE, PLANE, 3, 3)
        part = slice(half * PAIRS, (half + 1) * PAIRS)
        sent[part, :, :128] = main[:, :4].astype(BF)
        sent[part, :, 128:256] = main[:, 4:].astype(BF)
        sent[part, :, 256:] = more[:, :4].astype(BF)
        copy = pltpu.make_async_copy(sent.at[part], out.at[part], sems.at[6 + half])
        copy.start()
        outward.append(copy)
    for copy in outward:
        copy.wait()


def warp(shift, ids, raw, table, interpret=False):
    away = pl.BlockSpec(memory_space=pl.ANY)
    shape = (TILES, 4, 3 * 128)
    return pl.pallas_call(
        warp_kernel,
        out_shape=(
            jax.ShapeDtypeStruct(shape, BF),
            pltpu.VMEM((CH, DEPTH * ROWS, WIDTH), BF),
        ),
        in_specs=[pl.BlockSpec(memory_space=pltpu.SMEM), away, away, away],
        out_specs=(away, pl.BlockSpec(memory_space=pltpu.VMEM)),
        scratch_shapes=[
            pltpu.VMEM(raw.shape, BF),
            pltpu.VMEM(table.shape, BF),
            pltpu.SMEM(ids.shape, jnp.int32),
            pltpu.VMEM(shape, BF),
            pltpu.SemaphoreType.DMA((8,)),
        ],
        name="warp",
        interpret=interpret,
    )(shift, ids, raw, table)


def prepare_kernel(unmix, conv, bias, project, spread, banded, biases, projected):
    n = MIXED * ROWS
    k = iota((n, MIXED), 0)
    source = (k // PLANE % HALVES * FAR + k // (HALVES * PLANE)) * CH + k // ROWS % CH
    pick_in = (source == iota((n, MIXED), 1)).astype(BF)
    pick_out = (iota((MIXED, n), 1) % MIXED == iota((MIXED, n), 0)).astype(BF)
    tall = dot(pick_in, unmix[...], ((1,), (1,))).astype(BF)
    wide = dot(tall, pick_out, ((1,), (0,)))
    own = iota((n, n), 0) % ROWS == iota((n, n), 1) // MIXED
    spread[...] = jnp.where(own, wide, 0.0).astype(BF)
    gap = jnp.zeros((HIDDEN, MIXED), BF)
    for ab in range(9):
        at = (ab % 3 * 3 + ab // 3) * 256
        d = [conv[3 * ab + i] for i in range(3)]
        rows = [
            [d[1], d[2], gap, gap, gap, gap, gap, d[0]],
            [d[0], d[1], d[2], gap, gap, gap, gap, gap],
            [gap, d[0], d[1], d[2], gap, gap, gap, gap],
            [gap, gap, d[0], d[1], d[2], gap, gap, gap],
        ]
        for y in range(ROWS):
            banded[y * HIDDEN : (y + 1) * HIDDEN, at : at + 256] = jnp.concatenate(
                rows[y], axis=1
            )
    biases[...] = jnp.concatenate([bias[...]] * ROWS, axis=1)
    hole = jnp.zeros((MIXED, HIDDEN), BF)
    halved = (0.5 * project[...].astype(F32)).astype(BF)
    for y in range(ROWS):
        row = [halved if i == y else hole for i in range(ROWS)]
        projected[y * MIXED : (y + 1) * MIXED, :] = jnp.concatenate(row, axis=1)


def prepare(unmix, conv, bias, project, interpret=False):
    return pl.pallas_call(
        prepare_kernel,
        out_shape=(
            pltpu.VMEM((MIXED * ROWS, MIXED * ROWS), BF),
            jax.ShapeDtypeStruct((HIDDEN * ROWS, 9 * 256), BF),
            pltpu.VMEM((1, HIDDEN * ROWS), F32),
            pltpu.VMEM((MIXED * ROWS, HIDDEN * ROWS), BF),
        ),
        name="prepare",
        interpret=interpret,
    )(unmix, conv, bias, project)


def regroup_kernel(place, got, band, other, out, tall, sent, sems):
    thirds = [got[:, :, at : at + 128].astype(F32) for at in (0, 128, 256)]
    tall[...] = jnp.concatenate(thirds + thirds[2:], axis=1).reshape(TILES * 16, 128)

    def turn(a, b):
        rows = [tall[pl.ds(q, TILES, stride=16), :] for q in (a, b)]
        return jnp.concatenate(rows, axis=0).T

    turned = [turn(q, q + 1) for q in range(0, 12, 2)]
    first_half = place[0, :1, :128] == 0

    def piece(slot, column):
        x = column - 1
        inner = 1 <= slot <= 4
        if 0 <= x < 2 * BRICK:
            block, q = x // BRICK, x % BRICK
            if inner:
                which, start, at = q // 2, block * 64 + (slot - 1) * PLANE, q % 2 * 64
            else:
                which, start, at = 4, q * PLANE, block * 64
        else:
            side = 0 if x < 0 else 1
            if inner:
                which, start, at = 5, side * 64 + (slot - 1) * PLANE, 0
            else:
                which, start, at = 5, side * PLANE, 64
        rows = turned[which][start : start + PLANE]
        if not inner:
            keep = first_half if slot else jnp.logical_not(first_half)
            rows = jnp.where(keep, rows, 0.0)
        return rows, at

    refs = jnp.concatenate([band[...].astype(F32), other[...].astype(F32)], axis=0)
    marks = []
    for p in range(0, 8, 2):
        pair = refs[:, p * 64 : (p + 2) * 64]
        marks.append(jnp.concatenate([pltpu.roll(pair, 64, 1), pair], axis=0))
    lane = iota((PLANE, 128), 1)
    outward = []
    for core in range(2):
        for slot in range(6):
            pieces = [piece(slot, core * BRICK + k) for k in range(SPAN)]
            for half in range(HALVES):
                blocks = []
                for m in range(3):
                    block = jnp.zeros((PLANE, 128), F32)
                    for k in range(4 * m, min(4 * m + 4, SPAN)):
                        rows, at = pieces[k]
                        to = k % 4 * PAIRS
                        turn = (to - at - half * PAIRS) % 128
                        rows = pltpu.roll(rows, turn, 1) if turn else rows
                        block = jnp.where((lane >= to) & (lane < to + PAIRS), rows, block)
                    blocks.append(block)
                main = [block.astype(BF) for block in blocks[:2]]
                for far in range(FAR):
                    step = slot - far
                    if not 0 <= step < 3:
                        continue
                    w = step * HALVES + half
                    last = jnp.where(lane >= 64, marks[w], blocks[2]) if w < 4 else blocks[2]
                    rows = slice(w * PLANE, (w + 1) * PLANE)
                    sent[2 * far + core, rows, :128] = main[0]
                    sent[2 * far + core, rows, 128:256] = main[1]
                    sent[2 * far + core, rows, 256:] = last.astype(BF)
            if slot >= 2:
                peer = 2 * (slot - 2) + core
                copy = pltpu.make_async_copy(sent.at[peer], out.at[peer], sems.at[peer])
                copy.start()
                outward.append(copy)
    for copy in outward:
        copy.wait()


def regroup(place, got, band, other, interpret=False):
    shape = (2 * FAR, LINES, PADDED)
    return pl.pallas_call(
        regroup_kernel,
        out_shape=jax.ShapeDtypeStruct(shape, BF),
        in_specs=[pl.BlockSpec(memory_space=pltpu.VMEM)] * 4,
        out_specs=pl.BlockSpec(memory_space=pl.ANY),
        scratch_shapes=[
            pltpu.VMEM((TILES * 16, 128), F32),
            pltpu.VMEM(shape, BF),
            pltpu.SemaphoreType.DMA((2 * FAR,)),
        ],
        name="regroup",
        interpret=interpret,
    )(place, got, band, other)


def tables():
    x = np.arange(WIDTH, dtype=np.int64)
    half = WIDTH // 2
    frequency = np.where(x < half, x, np.where(x == half, half, x - half))
    angles = (x[:, None] * frequency[None, :] % WIDTH) * (2.0 * math.pi / WIDTH)
    table = np.where((x <= half)[None, :], np.cos(angles), np.sin(angles)).astype(np.float32)
    high = table.astype(jnp.bfloat16)
    low = (table - high.astype(np.float32)).astype(jnp.bfloat16)
    return high, low


def spectra_kernel(own, high, low, out):
    rows = own[...].reshape(CH * DEPTH * ROWS, WIDTH)
    out[...] = dot(rows, high[...], ((1,), (0,))) + dot(rows, low[...], ((1,), (0,)))


def own_spectra(own, high, low, interpret=False):
    return pl.pallas_call(
        spectra_kernel,
        out_shape=pltpu.VMEM((CH * DEPTH * ROWS, WIDTH), F32),
        name="spectra",
        interpret=interpret,
    )(own, high, low)


def correlate(place, own, got, high, low, out):
    half = WIDTH // 2
    count = CH * DEPTH * ROWS
    left = iota((2 * ROWS, 128), 1) < 64
    near, away = [], []
    for far in range(FAR):
        pieces = jnp.where(
            place[1, :1, :128] == 0,
            got[2 * far, :64, 256:].astype(F32),
            got[2 * far + 1, :64, 256:].astype(F32),
        )
        lanes = []
        for p in range(0, 8, 2):
            a = pieces[p * 2 * ROWS : (p + 1) * 2 * ROWS]
            b = pieces[(p + 1) * 2 * ROWS : (p + 2) * 2 * ROWS]
            lanes.append(jnp.where(left, pltpu.roll(a, 64, 1), b))
        rows = jnp.concatenate(lanes, axis=1)
        near.append(rows[:ROWS])
        away.append(rows[ROWS:])
    near, away = jnp.concatenate(near, axis=0), jnp.concatenate(away, axis=0)
    first_half = place[0, :1, :] == 0
    band = jnp.concatenate(
        [jnp.where(first_half, near, away), jnp.where(first_half, away, near)], axis=0
    ).astype(BF)
    along = ((1,), (0,))
    band = dot(band, high[...], along) + dot(band, low[...], along)
    own_cos = own[:, :half].reshape(CH, DEPTH * ROWS, half)
    own_sin = own[:, half:].reshape(CH, DEPTH * ROWS, half)
    band_cos = band[:, :half]
    band_sin = band[:, half:]
    first = iota(own_cos.shape, 2) == 0
    sines = own_sin * band_sin
    cosines = own_cos * band_cos
    real = jnp.where(first, cosines, 2.0 * (cosines + sines))
    imag = jnp.where(first, sines, 2.0 * (own_sin * band_cos - own_cos * band_sin))
    joined = jnp.concatenate([real.reshape(count, half), imag.reshape(count, half)], axis=1)
    upper = joined.astype(BF)
    lower = (joined - upper.astype(F32)).astype(BF)
    across = ((1,), (1,))
    both = dot(jnp.concatenate([upper, lower], axis=0), high[...], across)
    inverse = both[:count] + both[count:] + dot(upper, low[...], across)
    inverse = inverse * (1.0 / (WIDTH * math.sqrt(WIDTH)))
    for c in range(CH):
        for z in range(DEPTH):
            start = (c * DEPTH + z) * ROWS
            out[c, z] = inverse[start : start + ROWS]


def finish_kernel(
    place, own, got, high, low, spread, banded, biases, projected, away, out,
    found, wide, first, second, weights, sems,
):
    fetch = pltpu.make_async_copy(banded, weights, sems.at[0])
    fetch.start()
    correlate(place, own, got, high, low, found)
    leave = pltpu.make_async_copy(found, away, sems.at[1])
    leave.start()
    n = MIXED * ROWS
    pair = iota((SPAN, PAIRS, n), 1).reshape(ALONG, n)
    right = iota((ALONG, n), 1) >= 64
    count = BRICK * PAIRS
    centre = None
    for a in range(3):
        at = a * 256
        planes = []
        for core in range(2):
            mixed = jnp.concatenate(
                [
                    got[2 * far + core, a * HALVES * PLANE : (a + 1) * HALVES * PLANE, :]
                    for far in range(FAR)
                ],
                axis=0,
            )
            plane = dot(mixed, spread[...], ((0,), (0,)))[:ALONG].astype(BF)
            wide[core, :, at : at + 128] = plane
            planes.append(plane.astype(F32))
        even, odd = planes
        if a == 1:
            centre = jnp.concatenate([p[PAIRS : PAIRS + count] for p in planes], axis=0)
        upper = jnp.where(pair == 0, 0.0, pltpu.roll(odd, 1, 0))
        lower = jnp.where(pair == PAIRS - 1, 0.0, pltpu.roll(even, ALONG - 1, 0))
        wide[0, :, at + 128 : at + 256] = jnp.where(right, upper, odd).astype(BF)
        wide[1, :, at + 128 : at + 256] = jnp.where(right, even, lower).astype(BF)
    fetch.wait()
    total = biases[...]
    for b in range(3):
        rows = jnp.concatenate(
            [wide[core, b * PAIRS : b * PAIRS + count, :] for core in range(2)], axis=0
        )
        total = total + dot(rows, weights[:, b * 768 : (b + 1) * 768], ((1,), (1,)))
    slope = math.sqrt(2.0 / math.pi)
    hidden = total + total * jnp.tanh(total * (slope + slope * 0.044715 * (total * total)))
    hidden = hidden.astype(BF)
    mixed = dot(hidden, projected[...], ((1,), (1,)))
    done = centre + mixed
    left = iota((MIXED, 128), 1) < 64
    k = iota((256, 256), 0)
    order = iota((256, 256), 1) == 8 * (k % PAIRS) + 4 * (k // PAIRS % 2) + k // 64
    order = order.astype(BF)
    lines = []
    for x in range(0, BRICK, 2):
        pair = jnp.concatenate(
            [
                done[core * count + at * PAIRS : core * count + (at + 1) * PAIRS]
                for at in (x, x + 1)
                for core in range(2)
            ],
            axis=0,
        ).T
        y = [pair[i * MIXED : (i + 1) * MIXED, :] for i in range(ROWS)]
        lines.append(
            jnp.concatenate(
                [
                    jnp.where(left, y[0], pltpu.roll(y[1], 64, 1)),
                    jnp.where(left, y[2], pltpu.roll(y[3], 64, 1)),
                ],
                axis=1,
            )
        )
        lines.append(
            jnp.concatenate(
                [
                    jnp.where(left, pltpu.roll(y[0], 64, 1), y[1]),
                    jnp.where(left, pltpu.roll(y[2], 64, 1), y[3]),
                ],
                axis=1,
            )
        )
    ordered = dot(jnp.concatenate(lines, axis=0).astype(BF), order, ((1,), (0,)))
    for x in range(BRICK):
        rows = ordered[x * MIXED : (x + 1) * MIXED]
        first[pl.ds(x, MIXED, stride=BRICK), :] = rows[:, :128]
        second[pl.ds(x, MIXED, stride=BRICK), :] = rows[:, 128:]
    out[:, :, :128] = first[...].reshape(MIXED, BRICK, 128).astype(BF)
    out[:, :, 128:] = second[...].reshape(MIXED, BRICK, 128).astype(BF)
    leave.wait()


def finish(place, own, got, high, low, spread, banded, biases, projected, interpret=False):
    inside = pl.BlockSpec(memory_space=pltpu.VMEM)
    outside = pl.BlockSpec(memory_space=pl.ANY)
    found = (CH, DEPTH, ROWS, WIDTH)
    return pl.pallas_call(
        finish_kernel,
        in_specs=[inside] * 6 + [outside] + [inside] * 2,
        out_specs=(outside, inside),
        out_shape=(
            jax.ShapeDtypeStruct(found, F32),
            jax.ShapeDtypeStruct((MIXED, BRICK, TILES * ROWS), BF),
        ),
        scratch_shapes=[
            pltpu.VMEM(found, F32),
            pltpu.VMEM((2, ALONG, 3 * 256), BF),
            pltpu.VMEM((MIXED * BRICK, 128), F32),
            pltpu.VMEM((MIXED * BRICK, 128), F32),
            pltpu.VMEM(banded.shape, BF),
            pltpu.SemaphoreType.DMA((2,)),
        ],
        name="finish",
        interpret=interpret,
    )(place, own, got, high, low, spread, banded, biases, projected)


def close(value):
    return pltpu.with_memory_space_constraint(value, pltpu.VMEM)


def body(
    raw_tiles, ref_bands, shifts, matrix_ids, resample, unmix, conv_weight, conv_bias, out_weight
):
    high, low = tables()
    swap = functools.partial(
        lax.all_to_all, axis_name=("round", "tile"), split_axis=0, concat_axis=0, tiled=True
    )
    place = jnp.stack([lax.axis_index("round") >> 2, lax.axis_index("tile") & 1])
    place = close(jnp.broadcast_to(place[:, None, None], (2, 8, WIDTH)))
    band = close(ref_bands[0])
    ahead = [(i, (i + FAR) % ROUNDS) for i in range(ROUNDS)]
    other = close(lax.ppermute(band, "round", ahead))
    spread, banded, biases, projected = prepare(
        unmix, conv_weight, conv_bias.reshape(1, -1), out_weight
    )
    spread, biases, projected = map(close, (spread, biases, projected))
    high, low = close(jnp.asarray(high)), close(jnp.asarray(low))
    sent, own = warp(shifts, matrix_ids, raw_tiles[0], resample)
    got = close(swap(sent, axis_index_groups=RINGS))
    slabs = close(swap(regroup(place, got, band, other), axis_index_groups=NEAR))
    spectra = close(own_spectra(close(own), high, low))
    correlation, features = finish(
        place, spectra, slabs, high, low, spread, banded, biases, projected
    )
    return (correlation[None], features[:, None])


def solution(mesh):
    placed = (
        P("round", None, None, "tile", None),
        P("round", "tile", None),
        P("round", "tile"),
        P("round", None),
        P(),
        P(),
        P(),
        P(),
        P(),
    )
    return jax.shard_map(
        body,
        mesh=mesh,
        in_specs=placed,
        out_specs=(P("round", None, None, "tile", None), P(None, "round", "tile", None)),
        check_vma=False,
    )
```

```python
import functools
import math

import jax
import jax.numpy as jnp
import numpy as np
from jax import lax
from jax.experimental import pallas as pl
from jax.experimental.pallas import tpu as pltpu
from jax.sharding import PartitionSpec as P

BF = jnp.bfloat16
F32 = jnp.float32
ROUNDS, TILES = 8, 64
CH, DEPTH, ROWS, WIDTH = 4, 8, 4, 512
MIXED, HIDDEN = 32, 64
HALVES, FAR = 2, 4
PAIRS = TILES // 2
PLANE = CH * ROWS
BRICK = WIDTH // TILES
SPAN = BRICK + 2
BODY = 3 * HALVES * PLANE
LINES = BODY + 2 * PLANE + 2 * ROWS
ALONG = SPAN * PAIRS
PADDED = 256


def device(half, far, pair, core):
    return (half * FAR + far) * TILES + 2 * pair + core


RINGS = [
    [device(half, far, pair, core) for half in range(HALVES) for pair in range(PAIRS)]
    for far in range(FAR)
    for core in range(2)
]
NEAR = [
    [device(half, far, pair, core) for far in range(FAR) for core in range(2)]
    for half in range(HALVES)
    for pair in range(PAIRS)
]


def iota(shape, dim):
    return lax.broadcasted_iota(jnp.int32, shape, dim)


def dot(a, b, dims):
    return lax.dot_general(a, b, (dims, ((), ())), preferred_element_type=F32)


def warp_kernel(shift, ids, tiles, table, out, own, raw, mats, chosen, sent, sems):
    inward = [
        pltpu.make_async_copy(tiles, raw, sems.at[0]),
        pltpu.make_async_copy(ids, chosen, sems.at[1]),
    ]
    inward += [
        pltpu.make_async_copy(table.at[k], mats.at[k], sems.at[2 + k]) for k in range(len(mats))
    ]
    for copy in inward:
        copy.start()
    by = shift[0, 0]
    inward[0].wait()
    turned = []
    for c in range(CH):
        rows = jnp.concatenate([raw[c, z].astype(F32) for z in range(DEPTH)], axis=0)
        turned.append(pltpu.roll(rows, by, 1).astype(BF))
    for copy in inward[1:]:
        copy.wait()
    warped = []
    for c in range(CH):
        result = dot(turned[c], mats[chosen[0, c]], ((1,), (0,)))
        own[c] = result.astype(BF)
        warped.append(result.reshape(DEPTH // 2, 2 * ROWS, WIDTH))
    low = iota((DEPTH // 2, 2 * ROWS, WIDTH), 1) < ROWS
    even, odd = [], []
    for c in range(0, CH, 2):
        a, b = warped[c], warped[c + 1]
        even.append(jnp.where(low, a, pltpu.roll(b, ROWS, 1)))
        odd.append(jnp.where(low, pltpu.roll(a, ROWS, 1), b))
    planes = []
    for z in range(DEPTH):
        planes += [p[z // 2] for p in (odd if z % 2 else even)]
    upright = jnp.concatenate(planes, axis=0).T.reshape(PAIRS, 2, BRICK, DEPTH * PLANE)
    left, right = upright[:, 0], upright[:, 1]
    edge = jnp.zeros((1, BRICK, DEPTH * PLANE), F32)
    before = jnp.concatenate([edge, right[:-1]], axis=0)
    after = jnp.concatenate([left[1:], edge], axis=0)
    row, lane = iota(left.shape, 1), iota(left.shape, 2)

    def put(base, value, start, to, width, only=None, turn=0):
        value = pltpu.roll(value, turn, 1) if turn else value
        value = pltpu.roll(value, (to - start) % 128, 2) if to != start else value
        here = (lane >= to) & (lane < to + width)
        return jnp.where(here if only is None else here & (row == only), value, base)

    outward = []
    def gather(value, outer):
        turned = pltpu.roll(value, 128 - outer, 2)
        turned = pltpu.roll(turned, 0, 2, stride=PLANE, stride_axis=1)
        return jnp.sum(jnp.where(lane // PLANE == row, turned, 0.0), axis=1, keepdims=True)

    for half in range(HALVES):
        start = 64 * half
        main = put(left, right, start, 64, 64) if half == 0 else put(right, left, start, 0, 64)
        outer = 64 if half == 0 else 48
        more = jnp.where(row == 0, gather(left, outer), gather(right, outer))
        more = jnp.where(row < 2, more, 0.0)
        more = put(more, before, start, 0, 64, 2, 3)
        more = put(more, after, start, 64, 64, 2, 2)
        more = put(more, before, outer, 0, PLANE, 3, 4)
        more = put(more, after, outer, PLANE, PLANE, 3, 3)
        part = slice(half * PAIRS, (half + 1) * PAIRS)
        sent[part, :, :128] = main[:, :4].astype(BF)
        sent[part, :, 128:256] = main[:, 4:].astype(BF)
        sent[part, :, 256:] = more[:, :4].astype(BF)
        copy = pltpu.make_async_copy(sent.at[part], out.at[part], sems.at[6 + half])
        copy.start()
        outward.append(copy)
    for copy in outward:
        copy.wait()


def warp(shift, ids, raw, table, interpret=False):
    away = pl.BlockSpec(memory_space=pl.ANY)
    shape = (TILES, 4, 3 * 128)
    return pl.pallas_call(
        warp_kernel,
        out_shape=(
            jax.ShapeDtypeStruct(shape, BF),
            pltpu.VMEM((CH, DEPTH * ROWS, WIDTH), BF),
        ),
        in_specs=[pl.BlockSpec(memory_space=pltpu.SMEM), away, away, away],
        out_specs=(away, pl.BlockSpec(memory_space=pltpu.VMEM)),
        scratch_shapes=[
            pltpu.VMEM(raw.shape, BF),
            pltpu.VMEM(table.shape, BF),
            pltpu.SMEM(ids.shape, jnp.int32),
            pltpu.VMEM(shape, BF),
            pltpu.SemaphoreType.DMA((8,)),
        ],
        name="warp",
        interpret=interpret,
    )(shift, ids, raw, table)


def prepare_kernel(unmix, conv, bias, project, spread, banded, biases, projected):
    n = MIXED * ROWS
    k = iota((n, MIXED), 0)
    source = (k // PLANE % HALVES * FAR + k // (HALVES * PLANE)) * CH + k // ROWS % CH
    pick_in = (source == iota((n, MIXED), 1)).astype(BF)
    pick_out = (iota((MIXED, n), 1) % MIXED == iota((MIXED, n), 0)).astype(BF)
    tall = dot(pick_in, unmix[...], ((1,), (1,))).astype(BF)
    wide = dot(tall, pick_out, ((1,), (0,)))
    own = iota((n, n), 0) % ROWS == iota((n, n), 1) // MIXED
    spread[...] = jnp.where(own, wide, 0.0).astype(BF)
    gap = jnp.zeros((HIDDEN, MIXED), BF)
    for ab in range(9):
        at = (ab % 3 * 3 + ab // 3) * 256
        d = [conv[3 * ab + i] for i in range(3)]
        rows = [
            [d[1], d[2], gap, gap, gap, gap, gap, d[0]],
            [d[0], d[1], d[2], gap, gap, gap, gap, gap],
            [gap, d[0], d[1], d[2], gap, gap, gap, gap],
            [gap, gap, d[0], d[1], d[2], gap, gap, gap],
        ]
        for y in range(ROWS):
            banded[y * HIDDEN : (y + 1) * HIDDEN, at : at + 256] = jnp.concatenate(
                rows[y], axis=1
            )
    biases[...] = jnp.concatenate([bias[...]] * ROWS, axis=1)
    hole = jnp.zeros((MIXED, HIDDEN), BF)
    halved = (0.5 * project[...].astype(F32)).astype(BF)
    for y in range(ROWS):
        row = [halved if i == y else hole for i in range(ROWS)]
        projected[y * MIXED : (y + 1) * MIXED, :] = jnp.concatenate(row, axis=1)


def prepare(unmix, conv, bias, project, interpret=False):
    return pl.pallas_call(
        prepare_kernel,
        out_shape=(
            pltpu.VMEM((MIXED * ROWS, MIXED * ROWS), BF),
            jax.ShapeDtypeStruct((HIDDEN * ROWS, 9 * 256), BF),
            pltpu.VMEM((1, HIDDEN * ROWS), F32),
            pltpu.VMEM((MIXED * ROWS, HIDDEN * ROWS), BF),
        ),
        name="prepare",
        interpret=interpret,
    )(unmix, conv, bias, project)


def regroup_kernel(place, got, band, other, out, tall, sent, sems):
    thirds = [got[:, :, at : at + 128].astype(F32) for at in (0, 128, 256)]
    tall[...] = jnp.concatenate(thirds + thirds[2:], axis=1).reshape(TILES * 16, 128)

    def turn(a, b):
        rows = [tall[pl.ds(q, TILES, stride=16), :] for q in (a, b)]
        return jnp.concatenate(rows, axis=0).T

    turned = [turn(q, q + 1) for q in range(0, 12, 2)]
    first_half = place[0, :1, :128] == 0

    def piece(slot, column):
        x = column - 1
        inner = 1 <= slot <= 4
        if 0 <= x < 2 * BRICK:
            block, q = x // BRICK, x % BRICK
            if inner:
                which, start, at = q // 2, block * 64 + (slot - 1) * PLANE, q % 2 * 64
            else:
                which, start, at = 4, q * PLANE, block * 64
        else:
            side = 0 if x < 0 else 1
            if inner:
                which, start, at = 5, side * 64 + (slot - 1) * PLANE, 0
            else:
                which, start, at = 5, side * PLANE, 64
        rows = turned[which][start : start + PLANE]
        if not inner:
            keep = first_half if slot else jnp.logical_not(first_half)
            rows = jnp.where(keep, rows, 0.0)
        return rows, at

    refs = jnp.concatenate([band[...].astype(F32), other[...].astype(F32)], axis=0)
    marks = jnp.concatenate([refs[:, :128], refs[:, 128:256]], axis=0).astype(BF)
    marks_end = refs[:, 256:].astype(BF)
    lane = iota((PLANE, 128), 1)
    outward = []

    def place_pieces(pieces, half, block, first):
        for k, (rows, at) in enumerate(pieces):
            to = (first + k) * PAIRS
            turn = (to - at - half * PAIRS) % 128
            rows = pltpu.roll(rows, turn, 1) if turn else rows
            block = jnp.where((lane >= to) & (lane < to + PAIRS), rows, block)
        return block

    empty = jnp.zeros((PLANE, 128), F32)
    for core in range(2):
        for slot in range(6):
            pieces = [piece(slot, core * BRICK + k) for k in range(SPAN)]
            main = [
                [place_pieces(pieces[m : m + 4], half, empty, 0).astype(BF) for m in (0, 4)]
                for half in range(HALVES)
            ]
            tail = place_pieces(pieces[8:], 0, empty, 0)
            tail = place_pieces(pieces[8:], 1, tail, 2).astype(BF)
            for far in range(FAR):
                step = slot - far
                if not 0 <= step < 3:
                    continue
                peer = 2 * far + core
                for half in range(HALVES):
                    start = (step * HALVES + half) * PLANE
                    sent[peer, start : start + PLANE, :128] = main[half][0]
                    sent[peer, start : start + PLANE, 128:] = main[half][1]
                start = BODY + step // 2 * PLANE
                sent[peer, start : start + PLANE, step % 2 * 128 : (step % 2 + 1) * 128] = tail
            if slot >= 2:
                peer = 2 * (slot - 2) + core
                sent[peer, BODY + PLANE : BODY + 2 * PLANE, 128:] = marks
                sent[peer, BODY + 2 * PLANE :, :] = marks_end
                copy = pltpu.make_async_copy(sent.at[peer], out.at[peer], sems.at[peer])
                copy.start()
                outward.append(copy)
    for copy in outward:
        copy.wait()


def regroup(place, got, band, other, interpret=False):
    shape = (2 * FAR, LINES, PADDED)
    return pl.pallas_call(
        regroup_kernel,
        out_shape=jax.ShapeDtypeStruct(shape, BF),
        in_specs=[pl.BlockSpec(memory_space=pltpu.VMEM)] * 4,
        out_specs=pl.BlockSpec(memory_space=pl.ANY),
        scratch_shapes=[
            pltpu.VMEM((TILES * 16, 128), F32),
            pltpu.VMEM(shape, BF),
            pltpu.SemaphoreType.DMA((2 * FAR,)),
        ],
        name="regroup",
        interpret=interpret,
    )(place, got, band, other)


def tables():
    x = np.arange(WIDTH, dtype=np.int64)
    half = WIDTH // 2
    frequency = np.where(x < half, x, np.where(x == half, half, x - half))
    angles = (x[:, None] * frequency[None, :] % WIDTH) * (2.0 * math.pi / WIDTH)
    table = np.where((x <= half)[None, :], np.cos(angles), np.sin(angles)).astype(np.float32)
    high = table.astype(jnp.bfloat16)
    low = (table - high.astype(np.float32)).astype(jnp.bfloat16)
    return high, low


def spectra_kernel(own, high, low, out):
    rows = own[...].reshape(CH * DEPTH * ROWS, WIDTH)
    out[...] = dot(rows, high[...], ((1,), (0,))) + dot(rows, low[...], ((1,), (0,)))


def own_spectra(own, high, low, interpret=False):
    return pl.pallas_call(
        spectra_kernel,
        out_shape=pltpu.VMEM((CH * DEPTH * ROWS, WIDTH), F32),
        name="spectra",
        interpret=interpret,
    )(own, high, low)


def correlate(place, own, got, high, low, out):
    half = WIDTH // 2
    count = CH * DEPTH * ROWS
    mine = place[1, :1, :128] == 0
    near, away = [], []
    for far in range(FAR):
        a, b = got[2 * far, BODY + PLANE :, :], got[2 * far + 1, BODY + PLANE :, :]
        a, b = a.astype(F32), b.astype(F32)
        under = jnp.where(mine, a[:, :128], b[:, :128])
        top = jnp.where(mine, a[:, 128:], b[:, 128:])
        rows = jnp.concatenate(
            [
                top[: 2 * ROWS],
                top[2 * ROWS : 4 * ROWS],
                under[4 * ROWS :],
                top[4 * ROWS :],
            ],
            axis=1,
        )
        near.append(rows[:ROWS])
        away.append(rows[ROWS:])
    near, away = jnp.concatenate(near, axis=0), jnp.concatenate(away, axis=0)
    first_half = place[0, :1, :] == 0
    band = jnp.concatenate(
        [jnp.where(first_half, near, away), jnp.where(first_half, away, near)], axis=0
    ).astype(BF)
    along = ((1,), (0,))
    band = dot(band, high[...], along) + dot(band, low[...], along)
    own_cos = own[:, :half].reshape(CH, DEPTH * ROWS, half)
    own_sin = own[:, half:].reshape(CH, DEPTH * ROWS, half)
    band_cos = band[:, :half]
    band_sin = band[:, half:]
    first = iota(own_cos.shape, 2) == 0
    sines = own_sin * band_sin
    cosines = own_cos * band_cos
    real = jnp.where(first, cosines, 2.0 * (cosines + sines))
    imag = jnp.where(first, sines, 2.0 * (own_sin * band_cos - own_cos * band_sin))
    joined = jnp.concatenate([real.reshape(count, half), imag.reshape(count, half)], axis=1)
    upper = joined.astype(BF)
    lower = (joined - upper.astype(F32)).astype(BF)
    across = ((1,), (1,))
    both = dot(jnp.concatenate([upper, lower], axis=0), high[...], across)
    inverse = both[:count] + both[count:] + dot(upper, low[...], across)
    inverse = inverse * (1.0 / (WIDTH * math.sqrt(WIDTH)))
    for c in range(CH):
        for z in range(DEPTH):
            start = (c * DEPTH + z) * ROWS
            out[c, z] = inverse[start : start + ROWS]


def finish_kernel(
    place, own, got, high, low, spread, banded, biases, projected, away, out,
    found, wide, first, second, weights, sems,
):
    fetch = pltpu.make_async_copy(banded, weights, sems.at[0])
    fetch.start()
    correlate(place, own, got, high, low, found)
    leave = pltpu.make_async_copy(found, away, sems.at[1])
    leave.start()
    n = MIXED * ROWS
    pair = iota((SPAN, PAIRS, n), 1).reshape(ALONG, n)
    right = iota((ALONG, n), 1) >= 64
    count = BRICK * PAIRS
    centre = None
    for a in range(3):
        at = a * 256
        planes = []
        for core in range(2):
            inner = jnp.concatenate(
                [
                    got[2 * far + core, a * HALVES * PLANE : (a + 1) * HALVES * PLANE, :]
                    for far in range(FAR)
                ],
                axis=0,
            )
            tails = []
            for far in range(FAR):
                start = BODY + a // 2 * PLANE
                tail = got[
                    2 * far + core, start : start + PLANE, a % 2 * 128 : (a % 2 + 1) * 128
                ]
                tails += [tail, pltpu.roll(tail.astype(F32), 64, 1).astype(BF)]
            mixed = jnp.concatenate([inner, jnp.concatenate(tails, axis=0)], axis=1)
            plane = dot(mixed, spread[...], ((0,), (0,)))[:ALONG].astype(BF)
            wide[core, :, at : at + 128] = plane
            planes.append(plane.astype(F32))
        even, odd = planes
        if a == 1:
            centre = jnp.concatenate([p[PAIRS : PAIRS + count] for p in planes], axis=0)
        upper = jnp.where(pair == 0, 0.0, pltpu.roll(odd, 1, 0))
        lower = jnp.where(pair == PAIRS - 1, 0.0, pltpu.roll(even, ALONG - 1, 0))
        wide[0, :, at + 128 : at + 256] = jnp.where(right, upper, odd).astype(BF)
        wide[1, :, at + 128 : at + 256] = jnp.where(right, even, lower).astype(BF)
    fetch.wait()
    total = biases[...]
    for b in range(3):
        rows = jnp.concatenate(
            [wide[core, b * PAIRS : b * PAIRS + count, :] for core in range(2)], axis=0
        )
        total = total + dot(rows, weights[:, b * 768 : (b + 1) * 768], ((1,), (1,)))
    slope = math.sqrt(2.0 / math.pi)
    hidden = total + total * jnp.tanh(total * (slope + slope * 0.044715 * (total * total)))
    hidden = hidden.astype(BF)
    mixed = dot(hidden, projected[...], ((1,), (1,)))
    done = centre + mixed
    left = iota((MIXED, 128), 1) < 64
    k = iota((256, 256), 0)
    order = iota((256, 256), 1) == 8 * (k % PAIRS) + 4 * (k // PAIRS % 2) + k // 64
    order = order.astype(BF)
    lines = []
    for x in range(0, BRICK, 2):
        pair = jnp.concatenate(
            [
                done[core * count + at * PAIRS : core * count + (at + 1) * PAIRS]
                for at in (x, x + 1)
                for core in range(2)
            ],
            axis=0,
        ).T
        y = [pair[i * MIXED : (i + 1) * MIXED, :] for i in range(ROWS)]
        lines.append(
            jnp.concatenate(
                [
                    jnp.where(left, y[0], pltpu.roll(y[1], 64, 1)),
                    jnp.where(left, y[2], pltpu.roll(y[3], 64, 1)),
                ],
                axis=1,
            )
        )
        lines.append(
            jnp.concatenate(
                [
                    jnp.where(left, pltpu.roll(y[0], 64, 1), y[1]),
                    jnp.where(left, pltpu.roll(y[2], 64, 1), y[3]),
                ],
                axis=1,
            )
        )
    ordered = dot(jnp.concatenate(lines, axis=0).astype(BF), order, ((1,), (0,)))
    for x in range(BRICK):
        rows = ordered[x * MIXED : (x + 1) * MIXED]
        first[pl.ds(x, MIXED, stride=BRICK), :] = rows[:, :128]
        second[pl.ds(x, MIXED, stride=BRICK), :] = rows[:, 128:]
    out[:, :, :128] = first[...].reshape(MIXED, BRICK, 128).astype(BF)
    out[:, :, 128:] = second[...].reshape(MIXED, BRICK, 128).astype(BF)
    leave.wait()


def finish(place, own, got, high, low, spread, banded, biases, projected, interpret=False):
    inside = pl.BlockSpec(memory_space=pltpu.VMEM)
    outside = pl.BlockSpec(memory_space=pl.ANY)
    found = (CH, DEPTH, ROWS, WIDTH)
    return pl.pallas_call(
        finish_kernel,
        in_specs=[inside] * 6 + [outside] + [inside] * 2,
        out_specs=(outside, inside),
        out_shape=(
            jax.ShapeDtypeStruct(found, F32),
            jax.ShapeDtypeStruct((MIXED, BRICK, TILES * ROWS), BF),
        ),
        scratch_shapes=[
            pltpu.VMEM(found, F32),
            pltpu.VMEM((2, ALONG, 3 * 256), BF),
            pltpu.VMEM((MIXED * BRICK, 128), F32),
            pltpu.VMEM((MIXED * BRICK, 128), F32),
            pltpu.VMEM(banded.shape, BF),
            pltpu.SemaphoreType.DMA((2,)),
        ],
        name="finish",
        interpret=interpret,
    )(place, own, got, high, low, spread, banded, biases, projected)


def close(value):
    return pltpu.with_memory_space_constraint(value, pltpu.VMEM)


def body(
    raw_tiles, ref_bands, shifts, matrix_ids, resample, unmix, conv_weight, conv_bias, out_weight
):
    high, low = tables()
    swap = functools.partial(
        lax.all_to_all, axis_name=("round", "tile"), split_axis=0, concat_axis=0, tiled=True
    )
    place = jnp.stack([lax.axis_index("round") >> 2, lax.axis_index("tile") & 1])
    place = close(jnp.broadcast_to(place[:, None, None], (2, 8, WIDTH)))
    band = close(ref_bands[0])
    ahead = [(i, (i + FAR) % ROUNDS) for i in range(ROUNDS)]
    other = close(lax.ppermute(band, "round", ahead))
    spread, banded, biases, projected = prepare(
        unmix, conv_weight, conv_bias.reshape(1, -1), out_weight
    )
    spread, biases, projected = map(close, (spread, biases, projected))
    high, low = close(jnp.asarray(high)), close(jnp.asarray(low))
    sent, own = warp(shifts, matrix_ids, raw_tiles[0], resample)
    got = close(swap(sent, axis_index_groups=RINGS))
    slabs = close(swap(regroup(place, got, band, other), axis_index_groups=NEAR))
    spectra = close(own_spectra(close(own), high, low))
    correlation, features = finish(
        place, spectra, slabs, high, low, spread, banded, biases, projected
    )
    return (correlation[None], features[:, None])


def solution(mesh):
    placed = (
        P("round", None, None, "tile", None),
        P("round", "tile", None),
        P("round", "tile"),
        P("round", None),
        P(),
        P(),
        P(),
        P(),
        P(),
    )
    return jax.shard_map(
        body,
        mesh=mesh,
        in_specs=placed,
        out_specs=(P("round", None, None, "tile", None), P(None, "round", "tile", None)),
        check_vma=False,
    )
```
